32 devices in a mesh: parts: 2 (over y), inner: 4 (over z), outer: 2 (over x), rep: 2 (over core).
Axes of the slice: x: 2, y: 2, z: 4, core: 2. Of those that a mesh axis runs over, the one named last changes fastest.
Arguments:
- tokens: bfloat16 [512, 1024], P(('parts', 'inner', 'outer'), 'rep'), parts along dimension 0, may hold values from -6 to 6
- teacher: bfloat16 [512, 1024], P(('parts', 'inner', 'outer'), 'rep'), parts along dimension 0, may hold values from -1.5 to 1.5
- expert_ids: int32 [512, 8], P(('parts', 'inner', 'outer')), parts along dimension 0, may hold values from 0 to 7, as said below
- gate_codes: int32 [512, 8], P(('parts', 'inner', 'outer')), parts along dimension 0, may hold values from 49152 to 65535
- gate_up_latent: float32 [8, 2, 384, 1024], P(('inner', 'outer'), None, 'rep'), may hold values from -6 to 6
- down_latent: float32 [8, 384, 1024], P(('inner', 'outer'), 'rep'), may hold values from -6 to 6
Outputs:
- student_out: bfloat16 [512, 1024], P(('parts', 'inner', 'outer'), 'rep'), parts along dimension 0
- new_gate_up: float32 [16, 2, 384, 1024], P(('parts', 'inner', 'outer'), None, 'rep'), parts along dimension 0
- new_down: float32 [16, 384, 1024], P(('parts', 'inner', 'outer'), 'rep'), parts along dimension 0
The draws below stay inside these ranges and needn't reach their ends.
There are 2 independent parts, one for each index of `parts`. The reference program is written for one: setup_inputs(seed, part) draws one part's arguments, and reference() takes and returns one part's arrays. A program takes and returns all parts, laid end to end along the dimension named above; an argument that names none is the same for every part. Nothing has to cross between parts.
Inputs may be any that keep to these rules, and one draw needn't show every extreme that they name: `expert_ids`: each token names 8 different experts. Each aligned block of 32 tokens (the tokens of one device) names any expert at most 32 times, and one expert, the same in every block of a part, exactly 32 times in every block.
All inputs are finite; a program needn't handle non-finite values. Where the reference program divides by a largest or mean magnitude, that divisor is 1e-20 or more.
Results may differ from the reference program's by a relative error of at most 0.012.
Values may be sent and summed in bfloat16 or wider, within the bound.
No kernel may reach another device: no remote copies, remote signals or barrier semaphores. Data moves between devices by JAX's collectives and lax.ppermute only.
A program may use at most 64 MiB of HBM per device.

```python
import math
import jax
import jax.numpy as jnp
from jax import lax

D = 1024
HID = 384
TOPK = 8
TOK_DEV = 32
EXPERTS = 8
CAP = 32
TOKENS = 256
N_REP = 2


def draw_expert_ids(key, part):
    heat_level = jax.random.randint(jax.random.fold_in(key, 11), (EXPERTS,), 0, 4)
    hottest = jax.random.randint(jax.random.fold_in(key, 12), (), 0, EXPERTS)
    heat_level = jnp.where(jnp.arange(EXPERTS) == hottest, 5, heat_level)
    candidate = jnp.repeat(jnp.arange(EXPERTS, dtype=jnp.int32), CAP)
    priority = heat_level[candidate]
    pool_size = EXPERTS * CAP

    def draw_block(block_key):
        jitter = jax.random.randint(jax.random.fold_in(block_key, 1), (pool_size,), 0, 65536)
        scores = (priority * 65536 + jitter) * pool_size + jnp.arange(pool_size, dtype=jnp.int32)
        chosen = jnp.sort(candidate[lax.top_k(scores, TOK_DEV * TOPK)[1]])
        table = chosen.reshape(TOPK, TOK_DEV).T
        rotation = jax.random.randint(jax.random.fold_in(block_key, 2), (TOK_DEV, 1), 0, TOPK)
        column = (jnp.arange(TOPK, dtype=jnp.int32)[None, :] + rotation) % TOPK
        return jnp.take_along_axis(table, column, axis=1)
    block_keys = jax.random.split(jax.random.fold_in(key, 13), TOKENS // TOK_DEV)
    return jax.vmap(draw_block)(block_keys).reshape(TOKENS, TOPK).astype(jnp.int32)


def plant(array, rng, least, largest):
    index_at = [jax.random.randint(jax.random.fold_in(rng, axis), (), 0, length) for axis, length in enumerate(array.shape)]
    main_axis = array.shape.index(max(array.shape))
    beside = index_at[:main_axis] + [(index_at[main_axis] + 1) % array.shape[main_axis]] + index_at[main_axis + 1:]
    return array.at[tuple(index_at)].set(least).at[tuple(beside)].set(largest)


def shard_levels(rng, dims, cuts, least, high):
    level = 1.0
    for axis_at, shards_of in cuts:
        steps = jax.random.uniform(jax.random.fold_in(jax.random.fold_in(rng, 6), axis_at), (shards_of,), jnp.float32, least / len(cuts), high / len(cuts))
        level = level * jnp.repeat(jnp.exp(steps), dims[axis_at] // shards_of).reshape((-1,) + (1,) * (len(dims) - 1 - axis_at))
    return level


def noise(stream_key, shape, scale, reach, pieces=(), kind=jnp.bfloat16):
    array = jax.random.normal(stream_key, shape, jnp.float32) * scale
    if len(pieces) > 0:
        array = shard_levels(stream_key, shape, pieces, -0.22, 0.18) * array
    return jnp.clip(array, min=-reach, max=reach).astype(kind)


def setup_inputs(seed: int = 0, part: int = 0) -> dict:
    streams_of = jax.random.split(jax.random.key(seed), 7)
    part_keys = jax.random.split(jax.random.fold_in(streams_of[6], part), 7)
    tokens = noise(part_keys[0], (TOKENS, D), 1.0, 6.0, ((0, 8), (1, 2)))
    teacher = jnp.clip(jax.random.uniform(part_keys[1], (TOKENS, D), jnp.float32, -1.5, 1.5) * shard_levels(part_keys[1], (TOKENS, D), ((0, 8), (1, 2)), -0.4, 0.0), -1.5, 1.5).astype(jnp.bfloat16)
    expert_ids = draw_expert_ids(jax.random.fold_in(jax.random.fold_in(streams_of[6], part), 71), part)
    gate_codes = plant(jax.random.randint(part_keys[3], (TOKENS, TOPK), 49152, 65536), jax.random.fold_in(part_keys[3], 1), 49152, 65535).astype(jnp.int32)
    gate_up_latent = noise(streams_of[4], (EXPERTS, 2, HID, D), 1.0, 6.0, ((0, 8), (2, 2)), jnp.float32)
    down_latent = noise(streams_of[5], (EXPERTS, HID, D), 1.0, 6.0, ((0, 8), (1, 2)), jnp.float32)
    return dict(tokens=tokens, teacher=teacher, expert_ids=expert_ids, gate_codes=gate_codes, gate_up_latent=gate_up_latent, down_latent=down_latent)


learn_rate = 1.0

def soften(latent, fan_in):
    row_scale = lax.optimization_barrier(jnp.mean(jnp.abs(latent), axis=-1, keepdims=True)) + 1e-06
    normed = latent / row_scale
    lower = jnp.tanh(4.0 * (normed - 0.5))
    upper = jnp.tanh(4.0 * (normed + 0.5))
    fan_root = 1.0 / math.sqrt(fan_in)
    weight = (row_scale * 0.5 * (lower + upper) * fan_root).astype(jnp.bfloat16)
    slope = 2.0 * (2.0 - lower * lower - upper * upper) * fan_root
    return (weight, slope)

def expert_forward(gate_latent, down_part, inputs):
    gu_weight, gu_slope = soften(gate_latent, D)
    dn_weight, dn_slope = soften(down_part, HID)
    pre_gate = jnp.dot(gu_weight[0], inputs.T, preferred_element_type=jnp.float32)
    pre_up = jnp.dot(gu_weight[1], inputs.T, preferred_element_type=jnp.float32)
    sigmoid_gate = jax.nn.sigmoid(pre_gate)
    activated = pre_gate * sigmoid_gate
    hidden = (activated * pre_up).astype(jnp.bfloat16)
    return (gu_weight, gu_slope, dn_weight, dn_slope, pre_gate, pre_up, sigmoid_gate, activated, hidden)

def reference(tokens, teacher, expert_ids, gate_codes, gate_up_latent, down_latent):
    sources = TOKENS // TOK_DEV
    slot_rows = sources * CAP
    block_ids = expert_ids.reshape(sources, TOK_DEV * TOPK)
    one_hot = (block_ids[:, :, None] == jnp.arange(EXPERTS, dtype=jnp.int32)[None, None, :]).astype(jnp.int32)
    before = jnp.cumsum(one_hot, axis=1) - one_hot
    route_slot = lax.optimization_barrier(jnp.sum(before * one_hot, axis=2))
    source_index = jnp.arange(sources, dtype=jnp.int32)[:, None]
    target = (block_ids * slot_rows + source_index * CAP + route_slot).reshape(-1).astype(jnp.int32)
    routed = jnp.repeat(tokens, TOPK, axis=0)
    dispatched = jnp.zeros((EXPERTS * slot_rows, D), jnp.bfloat16).at[target].set(routed)
    dispatched = dispatched.reshape(EXPERTS, slot_rows, D)

    def forward(operands):
        gate_latent, down_part, inputs = operands
        parts = expert_forward(gate_latent, down_part, inputs)
        hidden = parts[8]
        dn_weight = parts[2]
        share_hidden = hidden.reshape(N_REP, HID // N_REP, -1).astype(jnp.float32)
        share_down = dn_weight.reshape(N_REP, HID // N_REP, D).astype(jnp.float32)
        shares = jnp.einsum('khr,khd->krd', share_hidden, share_down).astype(jnp.bfloat16)
        return lax.optimization_barrier(jnp.sum(shares.astype(jnp.float32), axis=0)).astype(jnp.bfloat16)
    expert_out = lax.map(forward, (gate_up_latent, down_latent, dispatched))
    gating = gate_codes.astype(jnp.float32) / 65536.0
    picked = expert_out.reshape(-1, D)[target].reshape(TOKENS, TOPK, D)
    mixed = lax.optimization_barrier(jnp.sum(gating[:, :, None] * picked.astype(jnp.float32), axis=1))
    student_out = mixed.astype(jnp.bfloat16)
    residual = mixed - teacher.astype(jnp.float32)
    pair_grad = (gating[:, :, None] * residual[:, None, :]).astype(jnp.bfloat16).reshape(-1, D)
    out_grad = jnp.zeros((EXPERTS * slot_rows, D), jnp.bfloat16).at[target].set(pair_grad)
    out_grad = out_grad.reshape(EXPERTS, slot_rows, D)

    def backward(operands):
        gate_latent, down_part, inputs, grads = operands
        gu_weight, gu_slope, dn_weight, dn_slope, pre_gate, pre_up, sigmoid_gate, activated, hidden = expert_forward(gate_latent, down_part, inputs)
        down_grad = jnp.dot(hidden, grads, preferred_element_type=jnp.float32)
        hidden_grad = jnp.dot(dn_weight, grads.T, preferred_element_type=jnp.float32)
        gate_grad = (hidden_grad * pre_up * sigmoid_gate * (1.0 + pre_gate * (1.0 - sigmoid_gate))).astype(jnp.bfloat16)
        up_grad = (hidden_grad * activated).astype(jnp.bfloat16)
        gate_wgrad = jnp.dot(gate_grad, inputs, preferred_element_type=jnp.float32)
        up_wgrad = jnp.dot(up_grad, inputs, preferred_element_type=jnp.float32)
        weight_grads = jnp.stack([gate_wgrad, up_wgrad])
        return (gate_latent - learn_rate * gu_slope * weight_grads, down_part - learn_rate * dn_slope * down_grad)
    new_gate_up, new_down = lax.map(backward, (gate_up_latent, down_latent, dispatched, out_grad))
    return (student_out, new_gate_up, new_down)
```

```python
import math

import jax
import jax.numpy as jnp
from jax import lax
from jax.sharding import PartitionSpec as P

learn_rate = 1.0


def soften(latent, fan_in):
    row_scale = jnp.mean(jnp.abs(latent), axis=-1, keepdims=True) + 1e-06
    normed = latent / row_scale
    lower = jnp.tanh(4.0 * (normed - 0.5))
    upper = jnp.tanh(4.0 * (normed + 0.5))
    fan_root = 1.0 / math.sqrt(fan_in)
    weight = (row_scale * 0.5 * (lower + upper) * fan_root).astype(jnp.bfloat16)
    slope = 2.0 * (2.0 - lower * lower - upper * upper) * fan_root
    return (weight, slope)


def shift(x, axis, step):
    size = lax.axis_size(axis)
    if step % size == 0:
        return x
    return lax.ppermute(x, axis, [(i, (i + step) % size) for i in range(size)])


def across(x, axis):
    return [shift(x, axis, k) for k in range(lax.axis_size(axis))]


def other_rep(x):
    return shift(x, "rep", 1)


def dense_step(tokens, teacher, expert_ids, gate_codes, gate_up_latent, down_latent):
    depth = lax.axis_size("inner")
    width = lax.axis_size("outer")
    reps = lax.axis_size("rep")
    experts = depth * width
    tok_rows, part_width = tokens.shape
    rep = lax.axis_index("rep")
    column_rows = depth * tok_rows

    chosen = expert_ids[:, :, None] == jnp.arange(experts, dtype=jnp.int32)[None, None, :]
    codes = jnp.sum(jnp.where(chosen, gate_codes[:, :, None], 0), axis=1).T

    def column(x, axis):
        return jnp.concatenate(across(x, "inner"), axis=axis)

    tok_column = column(tokens, 0)
    code_column = column(codes, 1)
    tok_rows_all = jnp.concatenate(across(tok_column, "outer"), axis=0)
    codes_all = jnp.concatenate(across(code_column, "outer"), axis=1)

    def both_features(x):
        theirs = other_rep(x)
        pair = jnp.where(rep == 0, jnp.stack([x, theirs]), jnp.stack([theirs, x]))
        return jnp.concatenate([pair[0], pair[1]], axis=1)

    expert_rows = both_features(tok_rows_all)
    mine = lax.axis_index("inner") * width + lax.axis_index("outer")
    gate = lax.dynamic_slice_in_dim(codes_all, mine, 1, 0).astype(jnp.float32) / 65536.0

    gu_weight, gu_slope = soften(gate_up_latent[0], tokens.shape[1] * reps)
    dn_weight, dn_slope = soften(down_latent[0], down_latent.shape[1] * reps)
    projected = lax.dot_general(
        gu_weight, expert_rows, (((2,), (1,)), ((), ())), preferred_element_type=jnp.float32
    )
    pre_gate = projected[0]
    pre_up = projected[1]
    sigmoid_gate = jax.nn.sigmoid(pre_gate)
    activated = pre_gate * sigmoid_gate
    gated_hidden = (activated * pre_up * gate).astype(jnp.bfloat16)

    dn_keep = lax.dynamic_slice_in_dim(dn_weight, rep * part_width, part_width, 1)
    dn_send = lax.dynamic_slice_in_dim(dn_weight, (1 - rep) * part_width, part_width, 1)

    def down(weight):
        return lax.dot_general(
            gated_hidden, weight, (((0,), (0,)), ((), ())), preferred_element_type=jnp.float32
        )

    theirs = other_rep(down(dn_send).astype(jnp.bfloat16))
    partial_out = down(dn_keep) + theirs.astype(jnp.float32)
    partial_out = partial_out.reshape(width, column_rows, part_width)
    column_sum = partial_out[0]
    for j in range(1, width):
        column_sum = column_sum + shift(partial_out[j].astype(jnp.bfloat16), "outer", -j).astype(
            jnp.float32
        )
    column_sum = column_sum.reshape(depth, tok_rows, part_width)
    mixed = column_sum[0]
    for k in range(1, depth):
        mixed = mixed + shift(column_sum[k].astype(jnp.bfloat16), "inner", -k).astype(jnp.float32)
    student_out = mixed.astype(jnp.bfloat16)
    residual = (mixed - teacher.astype(jnp.float32)).astype(jnp.bfloat16)

    res_rows = jnp.concatenate(across(column(residual, 0), "outer"), axis=0)
    upstream = both_features(res_rows)
    down_grad = jnp.dot(gated_hidden, upstream, preferred_element_type=jnp.float32)
    hidden_grad = gate * lax.dot_general(
        dn_weight, upstream, (((1,), (1,)), ((), ())), preferred_element_type=jnp.float32
    )
    gate_grad = (
        hidden_grad * pre_up * sigmoid_gate * (1.0 + pre_gate * (1.0 - sigmoid_gate))
    ).astype(jnp.bfloat16)
    up_grad = (hidden_grad * activated).astype(jnp.bfloat16)
    weight_grads = lax.dot_general(
        jnp.stack([gate_grad, up_grad]),
        expert_rows,
        (((2,), (0,)), ((), ())),
        preferred_element_type=jnp.float32,
    )
    new_gate_up = gate_up_latent - learn_rate * (gu_slope * weight_grads)[None]
    new_down = down_latent - learn_rate * (dn_slope * down_grad)[None]
    return (student_out, new_gate_up, new_down)


def exchange(outbox):
    return lax.all_to_all(outbox, ("inner", "outer"), split_axis=0, concat_axis=0, tiled=True)


def routed_step(tokens, teacher, expert_ids, gate_codes, gate_up_latent, down_latent):
    experts = lax.axis_size("inner") * lax.axis_size("outer")
    reps = lax.axis_size("rep")
    tok_rows, top_count = expert_ids.shape
    part_width = tokens.shape[1]
    capacity = min(tok_rows, 2 * tok_rows * top_count // experts)
    flat_ids = expert_ids.reshape(-1)
    one_hot = (flat_ids[:, None] == jnp.arange(experts, dtype=jnp.int32)[None, :]).astype(jnp.int32)
    before = jnp.cumsum(one_hot, axis=0) - one_hot
    route_slot = jnp.sum(before * one_hot, axis=1)
    target = flat_ids * capacity + route_slot
    payload = jnp.repeat(tokens, top_count, axis=0)
    outbox = jnp.zeros((experts * capacity, part_width), jnp.bfloat16).at[target].set(payload)
    received = exchange(outbox)
    expert_rows = lax.all_gather(received, "rep", axis=1, tiled=True)
    gu_weight, gu_slope = soften(gate_up_latent[0], part_width * reps)
    dn_weight, dn_slope = soften(down_latent[0], down_latent.shape[1] * reps)
    projected = lax.dot_general(
        gu_weight, expert_rows, (((2,), (1,)), ((), ())), preferred_element_type=jnp.float32
    )
    pre_gate = projected[0]
    pre_up = projected[1]
    sigmoid_gate = jax.nn.sigmoid(pre_gate)
    activated = pre_gate * sigmoid_gate
    hidden = (activated * pre_up).astype(jnp.bfloat16)
    partial_out = lax.dot_general(
        hidden, dn_weight, (((0,), (0,)), ((), ())), preferred_element_type=jnp.float32
    ).astype(jnp.bfloat16)
    rep = lax.axis_index("rep")
    keep = lax.dynamic_slice_in_dim(partial_out, rep * part_width, part_width, 1)
    send = lax.dynamic_slice_in_dim(partial_out, (1 - rep) * part_width, part_width, 1)
    expert_out = (keep.astype(jnp.float32) + other_rep(send).astype(jnp.float32)).astype(
        jnp.bfloat16
    )
    returned = exchange(expert_out)
    picked = returned[target].reshape(tok_rows, top_count, part_width)
    gating = gate_codes.astype(jnp.float32) / 65536.0
    mixed = jnp.sum(gating[:, :, None] * picked.astype(jnp.float32), axis=1)
    student_out = mixed.astype(jnp.bfloat16)
    residual = mixed - teacher.astype(jnp.float32)
    pair_grad = (
        (gating[:, :, None] * residual[:, None, :]).astype(jnp.bfloat16).reshape(-1, part_width)
    )
    grad_outbox = (
        jnp.zeros((experts * capacity, part_width), jnp.bfloat16).at[target].set(pair_grad)
    )
    grad_part = exchange(grad_outbox)
    out_grad = lax.all_gather(grad_part, "rep", axis=1, tiled=True)
    down_grad = jnp.dot(hidden, out_grad, preferred_element_type=jnp.float32)
    hidden_grad = lax.dot_general(
        dn_weight, out_grad, (((1,), (1,)), ((), ())), preferred_element_type=jnp.float32
    )
    gate_grad = (
        hidden_grad * pre_up * sigmoid_gate * (1.0 + pre_gate * (1.0 - sigmoid_gate))
    ).astype(jnp.bfloat16)
    up_grad = (hidden_grad * activated).astype(jnp.bfloat16)
    weight_grads = lax.dot_general(
        jnp.stack([gate_grad, up_grad]),
        expert_rows,
        (((2,), (0,)), ((), ())),
        preferred_element_type=jnp.float32,
    )
    new_gate_up = gate_up_latent - learn_rate * (gu_slope * weight_grads)[None]
    new_down = down_latent - learn_rate * (dn_slope * down_grad)[None]
    return (student_out, new_gate_up, new_down)


def on_device(tokens, teacher, expert_ids, gate_codes, gate_up_latent, down_latent):
    experts = lax.axis_size("inner") * lax.axis_size("outer")
    step = dense_step if expert_ids.shape[1] == experts else routed_step
    return step(tokens, teacher, expert_ids, gate_codes, gate_up_latent, down_latent)


def solution(mesh):
    return jax.shard_map(
        on_device,
        mesh=mesh,
        in_specs=(
            P(("parts", "inner", "outer"), "rep"),
            P(("parts", "inner", "outer"), "rep"),
            P(("parts", "inner", "outer"), None),
            P(("parts", "inner", "outer"), None),
            P(("inner", "outer"), None, "rep", None),
            P(("inner", "outer"), "rep", None),
        ),
        out_specs=(
            P(("parts", "inner", "outer"), "rep"),
            P(("parts", "inner", "outer"), None, "rep", None),
            P(("parts", "inner", "outer"), "rep", None),
        ),
        check_vma=False,
    )
```

```python
import math

import jax
import jax.numpy as jnp
from jax import lax
from jax.sharding import PartitionSpec as P

learn_rate = 1.0


def soften(latent, fan_in):
    row_scale = jnp.mean(jnp.abs(latent), axis=-1, keepdims=True) + 1e-06
    normed = latent / row_scale
    lower = jnp.tanh(4.0 * (normed - 0.5))
    upper = jnp.tanh(4.0 * (normed + 0.5))
    fan_root = 1.0 / math.sqrt(fan_in)
    weight = (row_scale * 0.5 * (lower + upper) * fan_root).astype(jnp.bfloat16)
    slope = 2.0 * (2.0 - lower * lower - upper * upper) * fan_root
    return (weight, slope)


def shift(x, axis, step):
    size = lax.axis_size(axis)
    if step % size == 0:
        return x
    return lax.ppermute(x, axis, [(i, (i + step) % size) for i in range(size)])


def across(x, axis):
    return [shift(x, axis, k) for k in range(lax.axis_size(axis))]


def other_rep(x):
    return shift(x, "rep", 1)


def exchange(outbox):
    return lax.all_to_all(outbox, ("inner", "outer"), split_axis=0, concat_axis=0, tiled=True)


def dense_step(tokens, teacher, expert_ids, gate_codes, gate_up_latent, down_latent):
    depth = lax.axis_size("inner")
    width = lax.axis_size("outer")
    reps = lax.axis_size("rep")
    tok_rows, part_width = tokens.shape
    rep = lax.axis_index("rep")
    inner = lax.axis_index("inner")
    outer = lax.axis_index("outer")
    f32 = jnp.float32
    bf16 = jnp.bfloat16

    def code_of(column):
        expert = (inner + jnp.arange(depth, dtype=jnp.int32)) % depth * width + column
        chosen = expert_ids[None] == expert[:, None, None]
        return jnp.sum(jnp.where(chosen, gate_codes[None], 0), axis=2)

    blocks = across(tokens, "inner")
    tok_groups = [jnp.concatenate(blocks, axis=0)]
    code_groups = [code_of(outer)]
    pad_rows = -depth % 8
    for j in range(1, width):
        codes = code_of((outer + j) % width)
        pieces = jnp.concatenate([codes // 256, codes % 256], axis=1).astype(bf16)
        pieces = jnp.pad(pieces, ((0, pad_rows), (0, part_width - 2 * tok_rows)))
        arrived = shift(jnp.concatenate([tok_groups[0], pieces], axis=0), "outer", j)
        tok_groups.append(arrived[: depth * tok_rows])
        pieces = arrived[depth * tok_rows : depth * tok_rows + depth].astype(f32)
        code_groups.append(256.0 * pieces[:, :tok_rows] + pieces[:, tok_rows : 2 * tok_rows])
    gate = jnp.concatenate([c.astype(f32) for c in code_groups], axis=1)[:, :, None] / 65536.0

    def both_features(x):
        theirs = other_rep(x)
        pair = jnp.where(rep == 0, jnp.stack([x, theirs]), jnp.stack([theirs, x]))
        return jnp.concatenate([pair[0], pair[1]], axis=1)

    expert_rows = jnp.concatenate([both_features(g) for g in tok_groups], axis=0)

    gu_weight, gu_slope = soften(gate_up_latent[0], tokens.shape[1] * reps)
    dn_weight, dn_slope = soften(down_latent[0], down_latent.shape[1] * reps)
    projected = lax.dot_general(
        gu_weight, expert_rows, (((2,), (1,)), ((), ())), preferred_element_type=f32
    )
    pre_gate = projected[0]
    pre_up = projected[1]
    sigmoid_gate = jax.nn.sigmoid(pre_gate)
    activated = pre_gate * sigmoid_gate
    hidden = (activated * pre_up).astype(bf16)

    dn_keep = lax.dynamic_slice_in_dim(dn_weight, rep * part_width, part_width, 1)
    dn_send = lax.dynamic_slice_in_dim(dn_weight, (1 - rep) * part_width, part_width, 1)

    def down(weight):
        return lax.dot_general(hidden, weight, (((0,), (0,)), ((), ())), preferred_element_type=f32)

    theirs = other_rep(down(dn_send).astype(bf16))
    expert_out = (down(dn_keep) + theirs.astype(f32)).astype(bf16)
    expert_out = expert_out.reshape(width, depth, tok_rows, part_width)

    pair_rows = width * tok_rows
    column_sum = 0.0
    for k in range(depth):
        picked = shift(expert_out[:, k].reshape(pair_rows, part_width), "inner", -k)
        column_sum = column_sum + gate[k] * picked.astype(f32)
    column_sum = column_sum.reshape(width, tok_rows, part_width)
    wanted = teacher.astype(f32)
    sent = jnp.concatenate([(column_sum[0] - wanted)[None], column_sum[1:]], axis=0).astype(bf16)
    sums = [column_sum[j] for j in range(width)]
    for step in range(1, width):
        arrived = shift(sent, "outer", step).astype(f32)
        sums = [sums[j] + arrived[(j - step) % width] for j in range(width)]
    student_out = sums[0].astype(bf16)
    residual = jnp.concatenate([sums[0] - wanted] + sums[1:], axis=0)
    grads = [shift((gate[k] * residual).astype(bf16), "inner", k) for k in range(depth)]
    grads = jnp.stack([g.reshape(width, tok_rows, part_width) for g in grads], axis=1)
    upstream = both_features(grads.reshape(depth * pair_rows, part_width))

    down_grad = jnp.dot(hidden, upstream, preferred_element_type=f32)
    hidden_grad = lax.dot_general(
        dn_weight, upstream, (((1,), (1,)), ((), ())), preferred_element_type=f32
    )
    gate_grad = (
        hidden_grad * pre_up * sigmoid_gate * (1.0 + pre_gate * (1.0 - sigmoid_gate))
    ).astype(bf16)
    up_grad = (hidden_grad * activated).astype(bf16)
    weight_grads = lax.dot_general(
        jnp.stack([gate_grad, up_grad]),
        expert_rows,
        (((2,), (0,)), ((), ())),
        preferred_element_type=f32,
    )
    new_gate_up = gate_up_latent - learn_rate * (gu_slope * weight_grads)[None]
    new_down = down_latent - learn_rate * (dn_slope * down_grad)[None]
    return (student_out, new_gate_up, new_down)


def routed_step(tokens, teacher, expert_ids, gate_codes, gate_up_latent, down_latent):
    experts = lax.axis_size("inner") * lax.axis_size("outer")
    reps = lax.axis_size("rep")
    tok_rows, top_count = expert_ids.shape
    part_width = tokens.shape[1]
    capacity = min(tok_rows, 2 * tok_rows * top_count // experts)
    flat_ids = expert_ids.reshape(-1)
    one_hot = (flat_ids[:, None] == jnp.arange(experts, dtype=jnp.int32)[None, :]).astype(jnp.int32)
    before = jnp.cumsum(one_hot, axis=0) - one_hot
    route_slot = jnp.sum(before * one_hot, axis=1)
    target = flat_ids * capacity + route_slot
    payload = jnp.repeat(tokens, top_count, axis=0)
    outbox = jnp.zeros((experts * capacity, part_width), jnp.bfloat16).at[target].set(payload)
    received = exchange(outbox)
    expert_rows = lax.all_gather(received, "rep", axis=1, tiled=True)
    gu_weight, gu_slope = soften(gate_up_latent[0], part_width * reps)
    dn_weight, dn_slope = soften(down_latent[0], down_latent.shape[1] * reps)
    projected = lax.dot_general(
        gu_weight, expert_rows, (((2,), (1,)), ((), ())), preferred_element_type=jnp.float32
    )
    pre_gate = projected[0]
    pre_up = projected[1]
    sigmoid_gate = jax.nn.sigmoid(pre_gate)
    activated = pre_gate * sigmoid_gate
    hidden = (activated * pre_up).astype(jnp.bfloat16)
    partial_out = lax.dot_general(
        hidden, dn_weight, (((0,), (0,)), ((), ())), preferred_element_type=jnp.float32
    ).astype(jnp.bfloat16)
    rep = lax.axis_index("rep")
    keep = lax.dynamic_slice_in_dim(partial_out, rep * part_width, part_width, 1)
    send = lax.dynamic_slice_in_dim(partial_out, (1 - rep) * part_width, part_width, 1)
    expert_out = (keep.astype(jnp.float32) + other_rep(send).astype(jnp.float32)).astype(
        jnp.bfloat16
    )
    returned = exchange(expert_out)
    picked = returned[target].reshape(tok_rows, top_count, part_width)
    gating = gate_codes.astype(jnp.float32) / 65536.0
    mixed = jnp.sum(gating[:, :, None] * picked.astype(jnp.float32), axis=1)
    student_out = mixed.astype(jnp.bfloat16)
    residual = mixed - teacher.astype(jnp.float32)
    pair_grad = (
        (gating[:, :, None] * residual[:, None, :]).astype(jnp.bfloat16).reshape(-1, part_width)
    )
    grad_outbox = (
        jnp.zeros((experts * capacity, part_width), jnp.bfloat16).at[target].set(pair_grad)
    )
    grad_part = exchange(grad_outbox)
    out_grad = lax.all_gather(grad_part, "rep", axis=1, tiled=True)
    down_grad = jnp.dot(hidden, out_grad, preferred_element_type=jnp.float32)
    hidden_grad = lax.dot_general(
        dn_weight, out_grad, (((1,), (1,)), ((), ())), preferred_element_type=jnp.float32
    )
    gate_grad = (
        hidden_grad * pre_up * sigmoid_gate * (1.0 + pre_gate * (1.0 - sigmoid_gate))
    ).astype(jnp.bfloat16)
    up_grad = (hidden_grad * activated).astype(jnp.bfloat16)
    weight_grads = lax.dot_general(
        jnp.stack([gate_grad, up_grad]),
        expert_rows,
        (((2,), (0,)), ((), ())),
        preferred_element_type=jnp.float32,
    )
    new_gate_up = gate_up_latent - learn_rate * (gu_slope * weight_grads)[None]
    new_down = down_latent - learn_rate * (dn_slope * down_grad)[None]
    return (student_out, new_gate_up, new_down)


def on_device(tokens, teacher, expert_ids, gate_codes, gate_up_latent, down_latent):
    experts = lax.axis_size("inner") * lax.axis_size("outer")
    step = dense_step if expert_ids.shape[1] == experts else routed_step
    return step(tokens, teacher, expert_ids, gate_codes, gate_up_latent, down_latent)


def solution(mesh):
    return jax.shard_map(
        on_device,
        mesh=mesh,
        in_specs=(
            P(("parts", "inner", "outer"), "rep"),
            P(("parts", "inner", "outer"), "rep"),
            P(("parts", "inner", "outer"), None),
            P(("parts", "inner", "outer"), None),
            P(("inner", "outer"), None, "rep", None),
            P(("inner", "outer"), "rep", None),
        ),
        out_specs=(
            P(("parts", "inner", "outer"), "rep"),
            P(("parts", "inner", "outer"), None, "rep", None),
            P(("parts", "inner", "outer"), "rep", None),
        ),
        check_vma=False,
    )
```

```python
import math

import jax
import jax.numpy as jnp
from jax import lax
from jax.experimental import pallas as pl
from jax.experimental.pallas import tpu as pltpu
from jax.sharding import PartitionSpec as P

learn_rate = 1.0


def soften(latent, fan_in):
    row_scale = jnp.mean(jnp.abs(latent), axis=-1, keepdims=True) + 1e-06
    steep = latent * (4.0 / row_scale)
    lower = jnp.tanh(steep - 2.0)
    upper = jnp.tanh(steep + 2.0)
    fan_root = 1.0 / math.sqrt(fan_in)
    weight = ((row_scale * (0.5 * fan_root)) * (lower + upper)).astype(jnp.bfloat16)
    slope = (4.0 * fan_root) - (2.0 * fan_root) * (lower * lower + upper * upper)
    return (weight, slope)


def ahead(place, step, size):
    return place ^ step if size & (size - 1) == 0 else (place + step) % size


def back(place, step, size):
    return place ^ step if size & (size - 1) == 0 else (place - step) % size


def shift(x, axis, step, way=ahead):
    size = lax.axis_size(axis)
    if step == 0:
        return x
    return lax.ppermute(x, axis, [(i, way(i, step, size)) for i in range(size)])


def in_order(size):
    return [k for k in (2, 1, 3) if k < size] + [0] + list(range(4, size))


def other_rep(x):
    return shift(x, "rep", 1)


def exchange(outbox):
    return lax.all_to_all(outbox, ("inner", "outer"), split_axis=0, concat_axis=0, tiled=True)


MEBI = 2**20


def dot(left, right, left_dim, right_dim):
    return lax.dot_general(
        left, right, (((left_dim,), (right_dim,)), ((), ())), preferred_element_type=jnp.float32
    )


def whole():
    return pl.BlockSpec(memory_space=pltpu.VMEM)


def like(shape, dtype):
    return jax.ShapeDtypeStruct(shape, dtype)


def halves(rep_ref, part_width):
    mine = pl.multiple_of(rep_ref[0] * part_width, part_width)
    theirs = pl.multiple_of((1 - rep_ref[0]) * part_width, part_width)
    return mine, theirs


def upright(gate):
    def body(flat, tall):
        tall[...] = flat[...].T

    return pl.pallas_call(
        body,
        in_specs=[whole()],
        out_specs=whole(),
        out_shape=like(gate.shape[::-1], gate.dtype),
        compiler_params=pltpu.CompilerParams(vmem_limit_bytes=2 * MEBI),
        name="upright",
    )(gate)


def soften_all(gate_up, down, gate_fan, down_fan):
    _, pair, hid, wide = gate_up.shape
    cuts = 2 if hid % 32 == 0 else 1
    rows = hid // cuts
    pieces = [(i, c) for i in range(pair + 1) for c in range(cuts)]

    def body(gu_ref, dn_ref, gu_weight, dn_weight, gu_slope, dn_slope, latent, sems):
        copies = []
        for n, (i, c) in enumerate(pieces):
            at = pl.ds(c * rows, rows)
            source = gu_ref.at[0, i, at] if i < pair else dn_ref.at[0, at]
            copies.append(pltpu.make_async_copy(source, latent.at[n], sems.at[n]))
            copies[-1].start()
        for n, (i, c) in enumerate(pieces):
            copies[n].wait()
            at = pl.ds(c * rows, rows)
            if i < pair:
                gu_weight[i, at], gu_slope[i, at] = soften(latent[n], gate_fan)
            else:
                dn_weight[at], dn_slope[at] = soften(latent[n], down_fan)

    return pl.pallas_call(
        body,
        in_specs=[pl.BlockSpec(memory_space=pltpu.HBM) for _ in range(2)],
        out_specs=[whole() for _ in range(4)],
        out_shape=[
            like((pair, hid, wide), jnp.bfloat16),
            like((hid, wide), jnp.bfloat16),
            like((pair, hid, wide), jnp.float32),
            like((hid, wide), jnp.float32),
        ],
        scratch_shapes=[
            pltpu.VMEM((len(pieces), rows, wide), jnp.float32),
            pltpu.SemaphoreType.DMA((len(pieces),)),
        ],
        compiler_params=pltpu.CompilerParams(vmem_limit_bytes=8 * MEBI),
        name="soften_all",
    )(pltpu.with_memory_space_constraint(gate_up, pltpu.HBM), pltpu.with_memory_space_constraint(down, pltpu.HBM))


def forward(rep, mine, theirs, gu_weight, dn_weight):
    hid = dn_weight.shape[0]
    rows, part = mine.shape

    def body(rep_ref, mine_ref, theirs_ref, gu_ref, dn_ref, hidden, by_gate, by_up, keep, send):
        here, there = halves(rep_ref, part)
        x_mine = mine_ref[...]
        x_theirs = theirs_ref[...]

        def project(which):
            return dot(gu_ref[which, :, pl.ds(here, part)], x_mine, 1, 1) + dot(
                gu_ref[which, :, pl.ds(there, part)], x_theirs, 1, 1
            )

        pre_gate = project(0)
        pre_up = project(1)
        sigmoid_gate = jax.nn.sigmoid(pre_gate)
        activated = pre_gate * sigmoid_gate
        rounded = (activated * pre_up).astype(jnp.bfloat16)
        send[...] = dot(rounded, dn_ref[:, pl.ds(there, part)], 0, 0).astype(jnp.bfloat16)
        keep[...] = dot(rounded, dn_ref[:, pl.ds(here, part)], 0, 0)
        hidden[...] = rounded
        by_gate[...] = pre_up * sigmoid_gate * (1.0 + pre_gate * (1.0 - sigmoid_gate))
        by_up[...] = activated

    return pl.pallas_call(
        body,
        in_specs=[pl.BlockSpec(memory_space=pltpu.SMEM)] + [whole() for _ in range(4)],
        out_specs=[whole() for _ in range(5)],
        out_shape=[
            like((hid, rows), jnp.bfloat16),
            like((hid, rows), jnp.float32),
            like((hid, rows), jnp.float32),
            like((rows, part), jnp.float32),
            like((rows, part), jnp.bfloat16),
        ],
        compiler_params=pltpu.CompilerParams(vmem_limit_bytes=8 * MEBI),
        name="forward",
    )(rep, mine, theirs, gu_weight, dn_weight)


def pack(keeps, arrivals, depth):
    width = len(keeps)
    rows, part = keeps[0].shape
    block = rows // depth

    def body(*refs):
        for j in range(width):
            total = (refs[j][...] + refs[width + j][...].astype(jnp.float32)).astype(jnp.bfloat16)
            for k in range(depth):
                refs[2 * width + k][j * block : (j + 1) * block, :] = total[
                    k * block : (k + 1) * block
                ]

    return pl.pallas_call(
        body,
        in_specs=[whole() for _ in range(2 * width)],
        out_specs=[whole() for _ in range(depth)],
        out_shape=[like((width * block, part), jnp.bfloat16) for _ in range(depth)],
        compiler_params=pltpu.CompilerParams(vmem_limit_bytes=4 * MEBI),
        name="pack",
    )(*keeps, *arrivals)


def mix(gate, picked, teacher):
    rows, part = picked[0].shape
    own = teacher.shape[0]

    def body(*refs):
        gate_ref, teacher_ref = refs[:2]
        total_ref, sent_ref = refs[-2:]
        gates = gate_ref[...]
        total = 0.0
        for k, ref in enumerate(refs[2:-2]):
            total = total + gates[:, k : k + 1] * ref[...].astype(jnp.float32)
        total_ref[...] = total
        sent_ref[:own, :] = (total[:own] - teacher_ref[...].astype(jnp.float32)).astype(
            jnp.bfloat16
        )
        sent_ref[own:, :] = total[own:].astype(jnp.bfloat16)

    return pl.pallas_call(
        body,
        in_specs=[whole() for _ in range(2 + len(picked))],
        out_specs=[whole(), whole()],
        out_shape=[like((rows, part), jnp.float32), like((rows, part), jnp.bfloat16)],
        compiler_params=pltpu.CompilerParams(vmem_limit_bytes=4 * MEBI),
        name="mix",
    )(gate, teacher, *picked)


def upstream(gate, total, arrivals, teacher, depth):
    rows, part = total.shape
    own = teacher.shape[0]
    width = rows // own

    def body(*refs):
        gate_ref, teacher_ref, total_ref = refs[:3]
        arrived = refs[3 : 3 + len(arrivals)]
        outs = refs[3 + len(arrivals) :]
        gates = gate_ref[...]
        for j in range(width):
            at = slice(j * own, (j + 1) * own)
            residual = total_ref[at, :]
            for step in range(1, width):
                source = back(j, step, width)
                residual = residual + arrived[step - 1][
                    source * own : (source + 1) * own, :
                ].astype(jnp.float32)
            if j == 0:
                residual = residual - teacher_ref[...].astype(jnp.float32)
            for k in range(depth):
                outs[k][at, :] = (gates[at, k : k + 1] * residual).astype(jnp.bfloat16)

    return pl.pallas_call(
        body,
        in_specs=[whole() for _ in range(3 + len(arrivals))],
        out_specs=[whole() for _ in range(depth)],
        out_shape=[like((rows, part), jnp.bfloat16) for _ in range(depth)],
        compiler_params=pltpu.CompilerParams(vmem_limit_bytes=4 * MEBI),
        name="upstream",
    )(gate, teacher, total, *arrivals)


def backward(rep, grads, rows_of, factors, weights, slopes, latents):
    gate_up, down = latents
    _, pair, hid, wide = gate_up.shape
    width = len(factors)
    depth = len(grads[0])
    part = grads[0][0].shape[1]
    block = grads[0][0].shape[0] // width
    flat = [*grads[0], grads[1], *rows_of[0], *rows_of[1]]
    for triple in factors:
        flat.extend(triple)
    flat.extend([weights, *slopes, gate_up, down])

    def body(*refs):
        refs = list(refs)
        rep_ref = refs.pop(0)
        mine_refs = [refs.pop(0) for _ in range(depth)]
        theirs_ref = refs.pop(0)
        x_mine = [refs.pop(0) for _ in range(width)]
        x_theirs = [refs.pop(0) for _ in range(width)]
        triples = [[refs.pop(0) for _ in range(3)] for _ in range(width)]
        dn_weight, gu_slope, dn_slope, gu_ref, dn_ref = [refs.pop(0) for _ in range(5)]
        gu_out, dn_out, gu_new, dn_new, sems = refs
        here, there = halves(rep_ref, part)
        at_of = (here, there)

        def group(which, j):
            at = slice(j * block, (j + 1) * block)
            if which == 0:
                return jnp.concatenate([ref[at, :] for ref in mine_refs], axis=0)
            rows = width * block
            return jnp.concatenate(
                [theirs_ref[k * rows + j * block : k * rows + (j + 1) * block, :] for k in range(depth)],
                axis=0,
            )

        groups = [[group(which, j) for j in range(width)] for which in range(2)]
        copies = []

        def send(source, target, sem):
            copy = pltpu.make_async_copy(source, target, sem)
            copy.start()
            copies.append(copy)

        for which in range(2):
            at = pl.ds(at_of[which], part)
            grad = sum(dot(triples[j][0][...], groups[which][j], 1, 0) for j in range(width))
            dn_new[which] = dn_ref[0, :, at] - dn_slope[:, at] * grad
            send(dn_new.at[which], dn_out.at[0, :, at], sems.at[2 * pair + which])
        row_grads = []
        for j in range(width):
            hidden_grad = dot(dn_weight[:, pl.ds(here, part)], groups[0][j], 1, 1) + dot(
                dn_weight[:, pl.ds(there, part)], groups[1][j], 1, 1
            )
            row_grads.append(
                [(hidden_grad * triples[j][1 + i][...]).astype(jnp.bfloat16) for i in range(pair)]
            )
        for i in range(pair):
            for which in range(2):
                at = pl.ds(at_of[which], part)
                rows = (x_mine, x_theirs)[which]
                grad = sum(dot(row_grads[j][i], rows[j][...], 1, 0) for j in range(width))
                gu_new[i, which] = gu_ref[0, i, :, at] - gu_slope[i, :, at] * grad
                send(gu_new.at[i, which], gu_out.at[0, i, :, at], sems.at[2 * i + which])
        for copy in copies:
            copy.wait()

    return pl.pallas_call(
        body,
        in_specs=[pl.BlockSpec(memory_space=pltpu.SMEM)] + [whole() for _ in flat],
        out_specs=[pl.BlockSpec(memory_space=pl.ANY), pl.BlockSpec(memory_space=pl.ANY)],
        out_shape=[like(gate_up.shape, jnp.float32), like(down.shape, jnp.float32)],
        scratch_shapes=[
            pltpu.VMEM((pair, 2, hid, part), jnp.float32),
            pltpu.VMEM((2, hid, part), jnp.float32),
            pltpu.SemaphoreType.DMA((2 * pair + 2,)),
        ],
        compiler_params=pltpu.CompilerParams(vmem_limit_bytes=8 * MEBI),
        name="backward",
    )(rep, *flat)


def dense_step(tokens, teacher, expert_ids, gate_codes, gate_up_latent, down_latent):
    depth = lax.axis_size("inner")
    width = lax.axis_size("outer")
    reps = lax.axis_size("rep")
    tok_rows, part_width = tokens.shape
    rep = lax.axis_index("rep").astype(jnp.int32)[None]
    inner = lax.axis_index("inner")
    outer = lax.axis_index("outer")
    f32 = jnp.float32
    bf16 = jnp.bfloat16
    tokens, rep, inner, outer = lax.optimization_barrier((tokens, rep, inner, outer))

    def over_inner(messages, way):
        arrived = {k: shift(messages[k], "inner", k, way) for k in in_order(depth)}
        return [arrived[k] for k in range(depth)]

    def code_of(column):
        expert = ahead(inner, jnp.arange(depth, dtype=jnp.int32), depth) * width + column
        chosen = expert_ids[None] == expert[:, None, None]
        return jnp.sum(jnp.where(chosen, gate_codes[None], 0), axis=2)

    blocks = over_inner([tokens] * depth, ahead)
    softened = soften_all(
        gate_up_latent, down_latent, part_width * reps, down_latent.shape[1] * reps
    )
    blocks[-1], *softened = lax.optimization_barrier((blocks[-1], *softened))
    gu_weight, dn_weight, gu_slope, dn_slope = softened

    tok_groups = [jnp.concatenate(blocks, axis=0)]
    code_groups = [code_of(outer)]
    pad_rows = -depth % 8
    for j in range(1, width):
        codes = code_of(ahead(outer, j, width))
        pieces = jnp.concatenate([codes // 256, codes % 256], axis=1).astype(bf16)
        pieces = jnp.pad(pieces, ((0, pad_rows), (0, part_width - 2 * tok_rows)))
        arrived = shift(jnp.concatenate([tok_groups[0], pieces], axis=0), "outer", j)
        tok_groups.append(arrived[: depth * tok_rows])
        pieces = arrived[depth * tok_rows : depth * tok_rows + depth].astype(f32)
        code_groups.append(256.0 * pieces[:, :tok_rows] + pieces[:, tok_rows : 2 * tok_rows])
    gate = jnp.concatenate([c.astype(f32) for c in code_groups], axis=1) / 65536.0
    gate = upright(jnp.pad(gate, ((0, -depth % 8), (0, -gate.shape[1] % 128))))
    gate = gate[: width * tok_rows]

    their_groups, factors, keeps, arrivals = [], [], [], []
    for group in tok_groups:
        theirs = other_rep(group)
        hidden, by_gate, by_up, keep, send = forward(rep, group, theirs, gu_weight, dn_weight)
        their_groups.append(theirs)
        factors.append((hidden, by_gate, by_up))
        keeps.append(keep)
        arrivals.append(other_rep(send))
    messages = pack(keeps, arrivals, depth)

    picked = over_inner(messages, back)
    total, sent = mix(gate, picked, teacher)
    arrivals = [shift(sent, "outer", step) for step in range(1, width)]
    outgoing = upstream(gate, total, arrivals, teacher, depth)
    grads = over_inner(outgoing, ahead)
    total, *arrivals, last = lax.optimization_barrier((total, *arrivals, grads[-1]))
    grads[-1] = last
    mixed = total[:tok_rows]
    for step in range(1, width):
        source = back(0, step, width)
        mixed = mixed + arrivals[step - 1][source * tok_rows : (source + 1) * tok_rows].astype(f32)
    student_out = mixed.astype(bf16)

    their_grads = other_rep(jnp.concatenate(grads, axis=0))
    new_gate_up, new_down = backward(
        rep,
        (grads, their_grads),
        (tok_groups, their_groups),
        factors,
        dn_weight,
        (gu_slope, dn_slope),
        (gate_up_latent, down_latent),
    )
    return (student_out, new_gate_up, new_down)


def routed_step(tokens, teacher, expert_ids, gate_codes, gate_up_latent, down_latent):
    experts = lax.axis_size("inner") * lax.axis_size("outer")
    reps = lax.axis_size("rep")
    tok_rows, top_count = expert_ids.shape
    part_width = tokens.shape[1]
    capacity = min(tok_rows, 2 * tok_rows * top_count // experts)
    flat_ids = expert_ids.reshape(-1)
    one_hot = (flat_ids[:, None] == jnp.arange(experts, dtype=jnp.int32)[None, :]).astype(jnp.int32)
    before = jnp.cumsum(one_hot, axis=0) - one_hot
    route_slot = jnp.sum(before * one_hot, axis=1)
    target = flat_ids * capacity + route_slot
    payload = jnp.repeat(tokens, top_count, axis=0)
    outbox = jnp.zeros((experts * capacity, part_width), jnp.bfloat16).at[target].set(payload)
    received = exchange(outbox)
    expert_rows = lax.all_gather(received, "rep", axis=1, tiled=True)
    gu_weight, gu_slope = soften(gate_up_latent[0], part_width * reps)
    dn_weight, dn_slope = soften(down_latent[0], down_latent.shape[1] * reps)
    projected = lax.dot_general(
        gu_weight, expert_rows, (((2,), (1,)), ((), ())), preferred_element_type=jnp.float32
    )
    pre_gate = projected[0]
    pre_up = projected[1]
    sigmoid_gate = jax.nn.sigmoid(pre_gate)
    activated = pre_gate * sigmoid_gate
    hidden = (activated * pre_up).astype(jnp.bfloat16)
    partial_out = lax.dot_general(
        hidden, dn_weight, (((0,), (0,)), ((), ())), preferred_element_type=jnp.float32
    ).astype(jnp.bfloat16)
    rep = lax.axis_index("rep")
    keep = lax.dynamic_slice_in_dim(partial_out, rep * part_width, part_width, 1)
    send = lax.dynamic_slice_in_dim(partial_out, (1 - rep) * part_width, part_width, 1)
    expert_out = (keep.astype(jnp.float32) + other_rep(send).astype(jnp.float32)).astype(
        jnp.bfloat16
    )
    returned = exchange(expert_out)
    picked = returned[target].reshape(tok_rows, top_count, part_width)
    gating = gate_codes.astype(jnp.float32) / 65536.0
    mixed = jnp.sum(gating[:, :, None] * picked.astype(jnp.float32), axis=1)
    student_out = mixed.astype(jnp.bfloat16)
    residual = mixed - teacher.astype(jnp.float32)
    pair_grad = (
        (gating[:, :, None] * residual[:, None, :]).astype(jnp.bfloat16).reshape(-1, part_width)
    )
    grad_outbox = (
        jnp.zeros((experts * capacity, part_width), jnp.bfloat16).at[target].set(pair_grad)
    )
    grad_part = exchange(grad_outbox)
    out_grad = lax.all_gather(grad_part, "rep", axis=1, tiled=True)
    down_grad = jnp.dot(hidden, out_grad, preferred_element_type=jnp.float32)
    hidden_grad = lax.dot_general(
        dn_weight, out_grad, (((1,), (1,)), ((), ())), preferred_element_type=jnp.float32
    )
    gate_grad = (
        hidden_grad * pre_up * sigmoid_gate * (1.0 + pre_gate * (1.0 - sigmoid_gate))
    ).astype(jnp.bfloat16)
    up_grad = (hidden_grad * activated).astype(jnp.bfloat16)
    weight_grads = lax.dot_general(
        jnp.stack([gate_grad, up_grad]),
        expert_rows,
        (((2,), (0,)), ((), ())),
        preferred_element_type=jnp.float32,
    )
    new_gate_up = gate_up_latent - learn_rate * (gu_slope * weight_grads)[None]
    new_down = down_latent - learn_rate * (dn_slope * down_grad)[None]
    return (student_out, new_gate_up, new_down)


def on_device(tokens, teacher, expert_ids, gate_codes, gate_up_latent, down_latent):
    experts = lax.axis_size("inner") * lax.axis_size("outer")
    step = dense_step if expert_ids.shape[1] == experts else routed_step
    return step(tokens, teacher, expert_ids, gate_codes, gate_up_latent, down_latent)


def solution(mesh):
    return jax.shard_map(
        on_device,
        mesh=mesh,
        in_specs=(
            P(("parts", "inner", "outer"), "rep"),
            P(("parts", "inner", "outer"), "rep"),
            P(("parts", "inner", "outer"), None),
            P(("parts", "inner", "outer"), None),
            P(("inner", "outer"), None, "rep", None),
            P(("inner", "outer"), "rep", None),
        ),
        out_specs=(
            P(("parts", "inner", "outer"), "rep"),
            P(("parts", "inner", "outer"), None, "rep", None),
            P(("parts", "inner", "outer"), "rep", None),
        ),
        check_vma=False,
    )
```

```python
import math

import jax
import jax.numpy as jnp
from jax import lax
from jax.experimental import pallas as pl
from jax.experimental.pallas import tpu as pltpu
from jax.sharding import PartitionSpec as P


learn_rate = 1.0


def soft_ternary(latent):
    row_scale = jnp.mean(jnp.abs(latent), axis=-1, keepdims=True) + 1e-06
    steep = latent * (4.0 / row_scale)
    return row_scale, jnp.tanh(steep - 2.0), jnp.tanh(steep + 2.0)


def weight_of(latent, fan_in):
    row_scale, lower, upper = soft_ternary(latent)
    return (row_scale * (0.5 / math.sqrt(fan_in)) * (lower + upper)).astype(jnp.bfloat16)


def slope_of(latent, fan_in):
    _, lower, upper = soft_ternary(latent)
    root = 2.0 / math.sqrt(fan_in)
    return 2.0 * root - root * (lower * lower + upper * upper)


def soften(latent, fan_in):
    return weight_of(latent, fan_in), slope_of(latent, fan_in)


def ahead(place, step, size):
    return place ^ step if size & (size - 1) == 0 else (place + step) % size


def back(place, step, size):
    return place ^ step if size & (size - 1) == 0 else (place - step) % size


def shift(x, axis, step, way=ahead):
    size = lax.axis_size(axis)
    if step == 0:
        return x
    return lax.ppermute(x, axis, [(i, way(i, step, size)) for i in range(size)])


def other_rep(x):
    return shift(x, "rep", 1)


def exchange(outbox):
    return lax.all_to_all(outbox, ("inner", "outer"), split_axis=0, concat_axis=0, tiled=True)


MEBI = 2**20


def dot(left, right, left_dim, right_dim):
    return lax.dot_general(
        left, right, (((left_dim,), (right_dim,)), ((), ())), preferred_element_type=jnp.float32
    )


def whole():
    return pl.BlockSpec(memory_space=pltpu.VMEM)


def like(shape, dtype):
    return jax.ShapeDtypeStruct(shape, dtype)


def halves(rep_ref, part_width):
    mine = pl.multiple_of(rep_ref[0] * part_width, part_width)
    theirs = pl.multiple_of((1 - rep_ref[0]) * part_width, part_width)
    return mine, theirs


def upright(gate):
    def body(flat, tall):
        tall[...] = flat[...].T

    return pl.pallas_call(
        body,
        in_specs=[whole()],
        out_specs=whole(),
        out_shape=like(gate.shape[::-1], gate.dtype),
        compiler_params=pltpu.CompilerParams(vmem_limit_bytes=2 * MEBI),
        name="upright",
    )(gate)


def per_entry(rule, latents, fans, dtype):
    pieces = []
    for n, latent in enumerate(latents):
        cuts = 2 if latent.shape[-2] % 32 == 0 else 1
        rows = latent.shape[-2] // cuts
        lead = [()]
        for size in latent.shape[:-2]:
            lead = [(*at, i) for at in lead for i in range(size)]
        pieces.extend((n, at, c * rows) for at in lead for c in range(cuts))
    wide = latents[0].shape[-1]

    def body(*refs):
        sources = refs[: len(latents)]
        targets = refs[len(latents) : -2]
        held, sems = refs[-2:]
        copies = []
        for slot, (n, at, row) in enumerate(pieces):
            source = sources[n].at[(*at, pl.ds(row, rows))]
            copies.append(pltpu.make_async_copy(source, held.at[slot], sems.at[slot]))
            copies[-1].start()
        for slot, (n, at, row) in enumerate(pieces):
            copies[slot].wait()
            targets[n][(*at, pl.ds(row, rows))] = rule(held[slot], fans[n])

    return pl.pallas_call(
        body,
        in_specs=[pl.BlockSpec(memory_space=pltpu.HBM) for _ in latents],
        out_specs=[whole() for _ in latents],
        out_shape=[like(latent.shape, dtype) for latent in latents],
        scratch_shapes=[
            pltpu.VMEM((len(pieces), rows, wide), jnp.float32),
            pltpu.SemaphoreType.DMA((len(pieces),)),
        ],
        compiler_params=pltpu.CompilerParams(vmem_limit_bytes=8 * MEBI),
    )(*[pltpu.with_memory_space_constraint(latent, pltpu.HBM) for latent in latents])


def forward(rep, mine, theirs, gu_weight, dn_weight):
    hid = dn_weight.shape[1]
    rows, part = mine.shape

    def body(rep_ref, mine_ref, theirs_ref, gu_ref, dn_ref, hidden, by_gate, by_up, keep, send):
        here, there = halves(rep_ref, part)
        x_mine = mine_ref[...]
        x_theirs = theirs_ref[...]

        def project(which):
            return dot(gu_ref[0, which, :, pl.ds(here, part)], x_mine, 1, 1) + dot(
                gu_ref[0, which, :, pl.ds(there, part)], x_theirs, 1, 1
            )

        pre_gate = project(0)
        pre_up = project(1)
        sigmoid_gate = jax.nn.sigmoid(pre_gate)
        activated = pre_gate * sigmoid_gate
        rounded = (activated * pre_up).astype(jnp.bfloat16)
        send[...] = dot(rounded, dn_ref[0, :, pl.ds(there, part)], 0, 0).astype(jnp.bfloat16)
        keep[...] = dot(rounded, dn_ref[0, :, pl.ds(here, part)], 0, 0)
        hidden[...] = rounded
        by_gate[...] = pre_up * sigmoid_gate * (1.0 + pre_gate * (1.0 - sigmoid_gate))
        by_up[...] = activated

    return pl.pallas_call(
        body,
        in_specs=[pl.BlockSpec(memory_space=pltpu.SMEM)] + [whole() for _ in range(4)],
        out_specs=[whole() for _ in range(5)],
        out_shape=[
            like((hid, rows), jnp.bfloat16),
            like((hid, rows), jnp.float32),
            like((hid, rows), jnp.float32),
            like((rows, part), jnp.float32),
            like((rows, part), jnp.bfloat16),
        ],
        compiler_params=pltpu.CompilerParams(vmem_limit_bytes=8 * MEBI),
        name="forward",
    )(rep, mine, theirs, gu_weight, dn_weight)


def pack(keeps, arrivals, depth):
    width = len(keeps)
    rows, part = keeps[0].shape
    block = rows // depth

    def body(*refs):
        for j in range(width):
            total = (refs[j][...] + refs[width + j][...].astype(jnp.float32)).astype(jnp.bfloat16)
            for k in range(depth):
                refs[2 * width + k][j * block : (j + 1) * block, :] = total[
                    k * block : (k + 1) * block
                ]

    return pl.pallas_call(
        body,
        in_specs=[whole() for _ in range(2 * width)],
        out_specs=[whole() for _ in range(depth)],
        out_shape=[like((width * block, part), jnp.bfloat16) for _ in range(depth)],
        compiler_params=pltpu.CompilerParams(vmem_limit_bytes=4 * MEBI),
        name="pack",
    )(*keeps, *arrivals)


def mix(gate, picked, teacher):
    rows, part = picked[0].shape
    own = teacher.shape[0]

    def body(*refs):
        gate_ref, teacher_ref = refs[:2]
        total_ref, sent_ref = refs[-2:]
        gates = gate_ref[...]
        total = 0.0
        for k, ref in enumerate(refs[2:-2]):
            total = total + gates[:, k : k + 1] * ref[...].astype(jnp.float32)
        total_ref[...] = total
        sent_ref[:own, :] = (total[:own] - teacher_ref[...].astype(jnp.float32)).astype(
            jnp.bfloat16
        )
        sent_ref[own:, :] = total[own:].astype(jnp.bfloat16)

    return pl.pallas_call(
        body,
        in_specs=[whole() for _ in range(2 + len(picked))],
        out_specs=[whole(), whole()],
        out_shape=[like((rows, part), jnp.float32), like((rows, part), jnp.bfloat16)],
        compiler_params=pltpu.CompilerParams(vmem_limit_bytes=4 * MEBI),
        name="mix",
    )(gate, teacher, *picked)


def upstream(gate, total, arrivals, teacher, depth):
    rows, part = total.shape
    own = teacher.shape[0]
    width = rows // own

    def body(*refs):
        gate_ref, teacher_ref, total_ref = refs[:3]
        arrived = refs[3 : 3 + len(arrivals)]
        outs = refs[3 + len(arrivals) :]
        gates = gate_ref[...]
        for j in range(width):
            at = slice(j * own, (j + 1) * own)
            residual = total_ref[at, :]
            for step in range(1, width):
                source = back(j, step, width)
                residual = residual + arrived[step - 1][
                    source * own : (source + 1) * own, :
                ].astype(jnp.float32)
            if j == 0:
                residual = residual - teacher_ref[...].astype(jnp.float32)
            for k in range(depth):
                outs[k][at, :] = (gates[at, k : k + 1] * residual).astype(jnp.bfloat16)

    return pl.pallas_call(
        body,
        in_specs=[whole() for _ in range(3 + len(arrivals))],
        out_specs=[whole() for _ in range(depth)],
        out_shape=[like((rows, part), jnp.bfloat16) for _ in range(depth)],
        compiler_params=pltpu.CompilerParams(vmem_limit_bytes=4 * MEBI),
        name="upstream",
    )(gate, teacher, total, *arrivals)


def backward(rep, grads, rows_of, factors, weights, slopes, latents):
    gate_up, down = latents
    _, pair, hid, _ = gate_up.shape
    width = len(factors)
    depth = len(grads[0])
    part = grads[0][0].shape[1]
    block = grads[0][0].shape[0] // width
    flat = [*grads[0], *grads[1], *rows_of[0], *rows_of[1]]
    for triple in factors:
        flat.extend(triple)
    flat.extend([weights, *slopes, gate_up, down])

    def body(*refs):
        refs = list(refs)
        rep_ref = refs.pop(0)
        mine_refs = [refs.pop(0) for _ in range(depth)]
        theirs_refs = [refs.pop(0) for _ in range(depth)]
        x_mine = [refs.pop(0) for _ in range(width)]
        x_theirs = [refs.pop(0) for _ in range(width)]
        triples = [[refs.pop(0) for _ in range(3)] for _ in range(width)]
        dn_weight, gu_slope, dn_slope, gu_ref, dn_ref = [refs.pop(0) for _ in range(5)]
        gu_out, dn_out, gu_new, dn_new, sems = refs
        here, there = halves(rep_ref, part)
        at_of = (here, there)

        def group(which, j):
            at = slice(j * block, (j + 1) * block)
            refs_of = (mine_refs, theirs_refs)[which]
            return jnp.concatenate([ref[at, :] for ref in refs_of], axis=0)

        groups = [[group(which, j) for j in range(width)] for which in range(2)]
        copies = []

        def send(source, target, sem):
            copy = pltpu.make_async_copy(source, target, sem)
            copy.start()
            copies.append(copy)

        for which in range(2):
            at = pl.ds(at_of[which], part)
            grad = sum(dot(triples[j][0][...], groups[which][j], 1, 0) for j in range(width))
            dn_new[which] = dn_ref[0, :, at] - dn_slope[0, :, at] * grad
            send(dn_new.at[which], dn_out.at[0, :, at], sems.at[2 * pair + which])
        row_grads = []
        for j in range(width):
            hidden_grad = dot(dn_weight[0, :, pl.ds(here, part)], groups[0][j], 1, 1) + dot(
                dn_weight[0, :, pl.ds(there, part)], groups[1][j], 1, 1
            )
            row_grads.append(
                [(hidden_grad * triples[j][1 + i][...]).astype(jnp.bfloat16) for i in range(pair)]
            )
        for i in range(pair):
            for which in range(2):
                at = pl.ds(at_of[which], part)
                rows = (x_mine, x_theirs)[which]
                grad = sum(dot(row_grads[j][i], rows[j][...], 1, 0) for j in range(width))
                gu_new[i, which] = gu_ref[0, i, :, at] - gu_slope[0, i, :, at] * grad
                send(gu_new.at[i, which], gu_out.at[0, i, :, at], sems.at[2 * i + which])
        for copy in copies:
            copy.wait()

    return pl.pallas_call(
        body,
        in_specs=[pl.BlockSpec(memory_space=pltpu.SMEM)] + [whole() for _ in flat],
        out_specs=[pl.BlockSpec(memory_space=pl.ANY), pl.BlockSpec(memory_space=pl.ANY)],
        out_shape=[like(gate_up.shape, jnp.float32), like(down.shape, jnp.float32)],
        scratch_shapes=[
            pltpu.VMEM((pair, 2, hid, part), jnp.float32),
            pltpu.VMEM((2, hid, part), jnp.float32),
            pltpu.SemaphoreType.DMA((2 * pair + 2,)),
        ],
        compiler_params=pltpu.CompilerParams(vmem_limit_bytes=8 * MEBI),
        name="backward",
    )(rep, *flat)


def dense_step(tokens, teacher, expert_ids, gate_codes, gate_up_latent, down_latent):
    depth = lax.axis_size("inner")
    width = lax.axis_size("outer")
    reps = lax.axis_size("rep")
    tok_rows, part_width = tokens.shape
    rep = lax.axis_index("rep").astype(jnp.int32)[None]
    inner = lax.axis_index("inner")
    outer = lax.axis_index("outer")
    f32 = jnp.float32
    bf16 = jnp.bfloat16
    tokens, rep, inner, outer = lax.optimization_barrier((tokens, rep, inner, outer))

    def over_inner(messages, way):
        arrived = []
        for k, message in enumerate(messages):
            arrived.append(shift(message, "inner", k, way))
        return arrived

    def code_of(column):
        expert = ahead(inner, jnp.arange(depth, dtype=jnp.int32), depth) * width + column
        chosen = expert_ids[None] == expert[:, None, None]
        return jnp.sum(jnp.where(chosen, gate_codes[None], 0), axis=2)

    blocks = over_inner([tokens] * depth, ahead)
    gate_fan = part_width * reps
    down_fan = down_latent.shape[1] * reps
    (gu_weight,) = per_entry(weight_of, [gate_up_latent], [gate_fan], bf16)
    blocks[-1], gu_weight = lax.optimization_barrier((blocks[-1], gu_weight))

    tok_groups = [jnp.concatenate(blocks, axis=0)]
    code_groups = [code_of(outer)]
    pad_rows = -depth % 8
    for j in range(1, width):
        codes = code_of(ahead(outer, j, width))
        pieces = jnp.concatenate([codes // 256, codes % 256], axis=1).astype(bf16)
        pieces = jnp.pad(pieces, ((0, pad_rows), (0, part_width - 2 * tok_rows)))
        arrived = shift(jnp.concatenate([tok_groups[0], pieces], axis=0), "outer", j)
        tok_groups.append(arrived[: depth * tok_rows])
        pieces = arrived[depth * tok_rows : depth * tok_rows + depth].astype(f32)
        code_groups.append(256.0 * pieces[:, :tok_rows] + pieces[:, tok_rows : 2 * tok_rows])
    gate = jnp.concatenate([c.astype(f32) for c in code_groups], axis=1) / 65536.0
    gate = upright(jnp.pad(gate, ((0, -depth % 8), (0, -gate.shape[1] % 128))))
    gate = gate[: width * tok_rows]

    (dn_weight,) = per_entry(weight_of, [down_latent], [down_fan], bf16)
    their_groups, factors, keeps, arrivals = [], [], [], []
    for group in tok_groups:
        theirs = other_rep(group)
        hidden, by_gate, by_up, keep, send = forward(rep, group, theirs, gu_weight, dn_weight)
        their_groups.append(theirs)
        factors.append((hidden, by_gate, by_up))
        keeps.append(keep)
        arrivals.append(other_rep(send))
    messages = list(pack(keeps, arrivals, depth))

    latents = [gate_up_latent, down_latent]
    messages[0], *latents = lax.optimization_barrier((messages[0], *latents))
    picked = over_inner(messages, back)
    slopes = per_entry(slope_of, latents, [gate_fan, down_fan], f32)
    picked[-1], *slopes = lax.optimization_barrier((picked[-1], *slopes))
    total, sent = mix(gate, picked, teacher)
    arrivals = [shift(sent, "outer", step) for step in range(1, width)]
    outgoing = upstream(gate, total, arrivals, teacher, depth)
    grads = over_inner(outgoing, ahead)
    total, *arrivals, last = lax.optimization_barrier((total, *arrivals, grads[-1]))
    grads[-1] = last
    mixed = total[:tok_rows]
    for step in range(1, width):
        source = back(0, step, width)
        mixed = mixed + arrivals[step - 1][source * tok_rows : (source + 1) * tok_rows].astype(f32)
    student_out = mixed.astype(bf16)

    their_grads = [other_rep(grad) for grad in grads]
    new_gate_up, new_down = backward(
        rep,
        (grads, their_grads),
        (tok_groups, their_groups),
        factors,
        dn_weight,
        slopes,
        latents,
    )
    return (student_out, new_gate_up, new_down)


def routed_step(tokens, teacher, expert_ids, gate_codes, gate_up_latent, down_latent):
    experts = lax.axis_size("inner") * lax.axis_size("outer")
    reps = lax.axis_size("rep")
    tok_rows, top_count = expert_ids.shape
    part_width = tokens.shape[1]
    capacity = min(tok_rows, 2 * tok_rows * top_count // experts)
    flat_ids = expert_ids.reshape(-1)
    one_hot = (flat_ids[:, None] == jnp.arange(experts, dtype=jnp.int32)[None, :]).astype(jnp.int32)
    before = jnp.cumsum(one_hot, axis=0) - one_hot
    route_slot = jnp.sum(before * one_hot, axis=1)
    target = flat_ids * capacity + route_slot
    payload = jnp.repeat(tokens, top_count, axis=0)
    outbox = jnp.zeros((experts * capacity, part_width), jnp.bfloat16).at[target].set(payload)
    received = exchange(outbox)
    expert_rows = lax.all_gather(received, "rep", axis=1, tiled=True)
    gu_weight, gu_slope = soften(gate_up_latent[0], part_width * reps)
    dn_weight, dn_slope = soften(down_latent[0], down_latent.shape[1] * reps)
    projected = lax.dot_general(
        gu_weight, expert_rows, (((2,), (1,)), ((), ())), preferred_element_type=jnp.float32
    )
    pre_gate = projected[0]
    pre_up = projected[1]
    sigmoid_gate = jax.nn.sigmoid(pre_gate)
    activated = pre_gate * sigmoid_gate
    hidden = (activated * pre_up).astype(jnp.bfloat16)
    partial_out = lax.dot_general(
        hidden, dn_weight, (((0,), (0,)), ((), ())), preferred_element_type=jnp.float32
    ).astype(jnp.bfloat16)
    rep = lax.axis_index("rep")
    keep = lax.dynamic_slice_in_dim(partial_out, rep * part_width, part_width, 1)
    send = lax.dynamic_slice_in_dim(partial_out, (1 - rep) * part_width, part_width, 1)
    expert_out = (keep.astype(jnp.float32) + other_rep(send).astype(jnp.float32)).astype(
        jnp.bfloat16
    )
    returned = exchange(expert_out)
    picked = returned[target].reshape(tok_rows, top_count, part_width)
    gating = gate_codes.astype(jnp.float32) / 65536.0
    mixed = jnp.sum(gating[:, :, None] * picked.astype(jnp.float32), axis=1)
    student_out = mixed.astype(jnp.bfloat16)
    residual = mixed - teacher.astype(jnp.float32)
    pair_grad = (
        (gating[:, :, None] * residual[:, None, :]).astype(jnp.bfloat16).reshape(-1, part_width)
    )
    grad_outbox = (
        jnp.zeros((experts * capacity, part_width), jnp.bfloat16).at[target].set(pair_grad)
    )
    grad_part = exchange(grad_outbox)
    out_grad = lax.all_gather(grad_part, "rep", axis=1, tiled=True)
    down_grad = jnp.dot(hidden, out_grad, preferred_element_type=jnp.float32)
    hidden_grad = lax.dot_general(
        dn_weight, out_grad, (((1,), (1,)), ((), ())), preferred_element_type=jnp.float32
    )
    gate_grad = (
        hidden_grad * pre_up * sigmoid_gate * (1.0 + pre_gate * (1.0 - sigmoid_gate))
    ).astype(jnp.bfloat16)
    up_grad = (hidden_grad * activated).astype(jnp.bfloat16)
    weight_grads = lax.dot_general(
        jnp.stack([gate_grad, up_grad]),
        expert_rows,
        (((2,), (0,)), ((), ())),
        preferred_element_type=jnp.float32,
    )
    new_gate_up = gate_up_latent - learn_rate * (gu_slope * weight_grads)[None]
    new_down = down_latent - learn_rate * (dn_slope * down_grad)[None]
    return (student_out, new_gate_up, new_down)


def on_device(tokens, teacher, expert_ids, gate_codes, gate_up_latent, down_latent):
    experts = lax.axis_size("inner") * lax.axis_size("outer")
    step = dense_step if expert_ids.shape[1] == experts else routed_step
    return step(tokens, teacher, expert_ids, gate_codes, gate_up_latent, down_latent)


def solution(mesh):
    return jax.shard_map(
        on_device,
        mesh=mesh,
        in_specs=(
            P(("parts", "inner", "outer"), "rep"),
            P(("parts", "inner", "outer"), "rep"),
            P(("parts", "inner", "outer"), None),
            P(("parts", "inner", "outer"), None),
            P(("inner", "outer"), None, "rep", None),
            P(("inner", "outer"), "rep", None),
        ),
        out_specs=(
            P(("parts", "inner", "outer"), "rep"),
            P(("parts", "inner", "outer"), None, "rep", None),
            P(("parts", "inner", "outer"), "rep", None),
        ),
        check_vma=False,
    )
```

```python
import math

import jax
import jax.numpy as jnp
from jax import lax
from jax.experimental import pallas as pl
from jax.experimental.pallas import tpu as pltpu
from jax.sharding import PartitionSpec as P


learn_rate = 1.0


def soft_ternary(latent):
    row_scale = jnp.mean(jnp.abs(latent), axis=-1, keepdims=True) + 1e-06
    steep = latent * (4.0 / row_scale)
    return row_scale, jnp.tanh(steep - 2.0), jnp.tanh(steep + 2.0)


def weight_of(latent, fan_in):
    row_scale, lower, upper = soft_ternary(latent)
    return (row_scale * (0.5 / math.sqrt(fan_in)) * (lower + upper)).astype(jnp.bfloat16)


def slope_of(latent, fan_in):
    _, lower, upper = soft_ternary(latent)
    root = 2.0 / math.sqrt(fan_in)
    return 2.0 * root - root * (lower * lower + upper * upper)


def soften(latent, fan_in):
    return weight_of(latent, fan_in), slope_of(latent, fan_in)


def ahead(place, step, size):
    return place ^ step if size & (size - 1) == 0 else (place + step) % size


def back(place, step, size):
    return place ^ step if size & (size - 1) == 0 else (place - step) % size


def shift(x, axis, step, way=ahead):
    size = lax.axis_size(axis)
    if step == 0:
        return x
    return lax.ppermute(x, axis, [(i, way(i, step, size)) for i in range(size)])


def other_rep(x):
    return shift(x, "rep", 1)


def exchange(outbox):
    return lax.all_to_all(outbox, ("inner", "outer"), split_axis=0, concat_axis=0, tiled=True)


MEBI = 2**20


def dot(left, right, left_dim, right_dim):
    return lax.dot_general(
        left, right, (((left_dim,), (right_dim,)), ((), ())), preferred_element_type=jnp.float32
    )


def whole():
    return pl.BlockSpec(memory_space=pltpu.VMEM)


def like(shape, dtype):
    return jax.ShapeDtypeStruct(shape, dtype)


def halves(rep_ref, part_width):
    mine = pl.multiple_of(rep_ref[0] * part_width, part_width)
    theirs = pl.multiple_of((1 - rep_ref[0]) * part_width, part_width)
    return mine, theirs


def upright(gate):
    def body(flat, tall):
        tall[...] = flat[...].T

    return pl.pallas_call(
        body,
        in_specs=[whole()],
        out_specs=whole(),
        out_shape=like(gate.shape[::-1], gate.dtype),
        compiler_params=pltpu.CompilerParams(vmem_limit_bytes=2 * MEBI),
        name="upright",
    )(gate)


def per_entry(rule, latents, fans, dtype, carried=()):
    pieces = []
    for n, latent in enumerate(latents):
        cuts = 2 if latent.shape[-2] % 32 == 0 else 1
        rows = latent.shape[-2] // cuts
        lead = [()]
        for size in latent.shape[:-2]:
            lead = [(*at, i) for at in lead for i in range(size)]
        pieces.extend((n, at, c * rows) for at in lead for c in range(cuts))
    wide = latents[0].shape[-1]

    def body(*refs):
        count = len(latents) + len(carried)
        sources = refs[:count]
        targets = refs[count:-2]
        held, sems = refs[-2:]
        copies = []
        for n in range(len(latents), count):
            sem = sems.at[len(pieces) + n - len(latents)]
            copies.append(pltpu.make_async_copy(sources[n], targets[n], sem))
            copies[-1].start()
        for slot, (n, at, row) in enumerate(pieces):
            source = sources[n].at[(*at, pl.ds(row, rows))]
            copies.append(pltpu.make_async_copy(source, held.at[slot], sems.at[slot]))
            copies[-1].start()
        for slot, (n, at, row) in enumerate(pieces):
            copies[len(carried) + slot].wait()
            targets[n][(*at, pl.ds(row, rows))] = rule(held[slot], fans[n])
        for copy in copies[: len(carried)]:
            copy.wait()

    inputs = [*latents, *carried]
    return pl.pallas_call(
        body,
        in_specs=[pl.BlockSpec(memory_space=pltpu.HBM) for _ in inputs],
        out_specs=[whole() for _ in inputs],
        out_shape=[like(latent.shape, dtype) for latent in latents]
        + [like(array.shape, array.dtype) for array in carried],
        scratch_shapes=[
            pltpu.VMEM((len(pieces), rows, wide), jnp.float32),
            pltpu.SemaphoreType.DMA((len(pieces) + len(carried),)),
        ],
        compiler_params=pltpu.CompilerParams(vmem_limit_bytes=8 * MEBI),
    )(*[pltpu.with_memory_space_constraint(array, pltpu.HBM) for array in inputs])


def project(rep, mine, gu_weight):
    pair, hid = gu_weight.shape[1:3]
    rows, part = mine.shape

    def body(rep_ref, mine_ref, gu_ref, out):
        here, _ = halves(rep_ref, part)
        for i in range(pair):
            out[i] = dot(gu_ref[0, i, :, pl.ds(here, part)], mine_ref[...], 1, 1)

    return pl.pallas_call(
        body,
        in_specs=[pl.BlockSpec(memory_space=pltpu.SMEM), whole(), whole()],
        out_specs=whole(),
        out_shape=like((pair, hid, rows), jnp.float32),
        compiler_params=pltpu.CompilerParams(vmem_limit_bytes=4 * MEBI),
        name="project",
    )(rep, mine, gu_weight)


def forward(rep, started, theirs, gu_weight, dn_weight):
    hid = dn_weight.shape[1]
    rows, part = theirs.shape
    pair = gu_weight.shape[1]

    def body(rep_ref, started_ref, theirs_ref, gu_ref, dn_ref, pre, hidden, send):
        _, there = halves(rep_ref, part)
        at = pl.ds(there, part)
        for i in range(pair):
            pre[i] = started_ref[i] + dot(gu_ref[0, i, :, at], theirs_ref[...], 1, 1)
        pre_gate = pre[0]
        rounded = (pre_gate * jax.nn.sigmoid(pre_gate) * pre[1]).astype(jnp.bfloat16)
        hidden[...] = rounded
        send[...] = dot(rounded, dn_ref[0, :, at], 0, 0).astype(jnp.bfloat16)

    return pl.pallas_call(
        body,
        in_specs=[pl.BlockSpec(memory_space=pltpu.SMEM)] + [whole() for _ in range(4)],
        out_specs=[whole() for _ in range(3)],
        out_shape=[
            like((pair, hid, rows), jnp.float32),
            like((hid, rows), jnp.bfloat16),
            like((rows, part), jnp.bfloat16),
        ],
        compiler_params=pltpu.CompilerParams(vmem_limit_bytes=8 * MEBI),
        name="forward",
    )(rep, started, theirs, gu_weight, dn_weight)


def keep_share(rep, pre, hidden, dn_weight):
    hid, rows = hidden.shape
    part = dn_weight.shape[2] // 2

    def body(rep_ref, pre_ref, hidden_ref, dn_ref, keep, by_gate, by_up):
        here, _ = halves(rep_ref, part)
        keep[...] = dot(hidden_ref[...], dn_ref[0, :, pl.ds(here, part)], 0, 0)
        pre_gate = pre_ref[0]
        sigmoid_gate = jax.nn.sigmoid(pre_gate)
        by_gate[...] = pre_ref[1] * sigmoid_gate * (1.0 + pre_gate * (1.0 - sigmoid_gate))
        by_up[...] = pre_gate * sigmoid_gate

    return pl.pallas_call(
        body,
        in_specs=[pl.BlockSpec(memory_space=pltpu.SMEM)] + [whole() for _ in range(3)],
        out_specs=[whole() for _ in range(3)],
        out_shape=[
            like((rows, part), jnp.float32),
            like((hid, rows), jnp.float32),
            like((hid, rows), jnp.float32),
        ],
        compiler_params=pltpu.CompilerParams(vmem_limit_bytes=8 * MEBI),
        name="keep_share",
    )(rep, pre, hidden, dn_weight)


def pack(keeps, arrivals, depth):
    width = len(keeps)
    rows, part = keeps[0].shape
    block = rows // depth

    def body(*refs):
        for j in range(width):
            total = (refs[j][...] + refs[width + j][...].astype(jnp.float32)).astype(jnp.bfloat16)
            for k in range(depth):
                refs[2 * width + k][j * block : (j + 1) * block, :] = total[
                    k * block : (k + 1) * block
                ]

    return pl.pallas_call(
        body,
        in_specs=[whole() for _ in range(2 * width)],
        out_specs=[whole() for _ in range(depth)],
        out_shape=[like((width * block, part), jnp.bfloat16) for _ in range(depth)],
        compiler_params=pltpu.CompilerParams(vmem_limit_bytes=4 * MEBI),
        name="pack",
    )(*keeps, *arrivals)


def mix(gate, picked, teacher):
    rows, part = picked[0].shape
    own = teacher.shape[0]

    def body(*refs):
        gate_ref, teacher_ref = refs[:2]
        total_ref, sent_ref = refs[-2:]
        gates = gate_ref[...]
        total = 0.0
        for k, ref in enumerate(refs[2:-2]):
            total = total + gates[:, k : k + 1] * ref[...].astype(jnp.float32)
        total_ref[...] = total
        sent_ref[:own, :] = (total[:own] - teacher_ref[...].astype(jnp.float32)).astype(
            jnp.bfloat16
        )
        sent_ref[own:, :] = total[own:].astype(jnp.bfloat16)

    return pl.pallas_call(
        body,
        in_specs=[whole() for _ in range(2 + len(picked))],
        out_specs=[whole(), whole()],
        out_shape=[like((rows, part), jnp.float32), like((rows, part), jnp.bfloat16)],
        compiler_params=pltpu.CompilerParams(vmem_limit_bytes=4 * MEBI),
        name="mix",
    )(gate, teacher, *picked)


def upstream(gate, total, arrivals, teacher, depth):
    rows, part = total.shape
    own = teacher.shape[0]
    width = rows // own

    def body(*refs):
        gate_ref, teacher_ref, total_ref = refs[:3]
        arrived = refs[3 : 3 + len(arrivals)]
        outs = refs[3 + len(arrivals) :]
        gates = gate_ref[...]
        for j in range(width):
            at = slice(j * own, (j + 1) * own)
            residual = total_ref[at, :]
            for step in range(1, width):
                source = back(j, step, width)
                residual = residual + arrived[step - 1][
                    source * own : (source + 1) * own, :
                ].astype(jnp.float32)
            if j == 0:
                residual = residual - teacher_ref[...].astype(jnp.float32)
            for k in range(depth):
                outs[k][at, :] = (gates[at, k : k + 1] * residual).astype(jnp.bfloat16)

    return pl.pallas_call(
        body,
        in_specs=[whole() for _ in range(3 + len(arrivals))],
        out_specs=[whole() for _ in range(depth)],
        out_shape=[like((rows, part), jnp.bfloat16) for _ in range(depth)],
        compiler_params=pltpu.CompilerParams(vmem_limit_bytes=4 * MEBI),
        name="upstream",
    )(gate, teacher, total, *arrivals)


def joined(refs, block, width):
    return jnp.concatenate(
        [ref[j * block : (j + 1) * block, :] for j in range(width) for ref in refs], axis=0
    )


def begin(rep, grads, hiddens, weight, slope, latent):
    hid = latent.shape[1]
    width = len(hiddens)
    depth = len(grads)
    block = grads[0].shape[0] // width
    part = grads[0].shape[1]
    rows = width * depth * block

    def body(rep_ref, *refs):
        grad_refs = refs[:depth]
        hidden_refs = refs[depth : depth + width]
        weight_ref, slope_ref, latent_ref, hidden_grad, new_down = refs[depth + width :]
        here, _ = halves(rep_ref, part)
        at = pl.ds(here, part)
        mine = joined(grad_refs, block, width)
        hidden_grad[...] = dot(weight_ref[0, :, at], mine, 1, 1)
        hidden = jnp.concatenate([ref[...] for ref in hidden_refs], axis=1)
        new_down[...] = latent_ref[0, :, at] - slope_ref[0, :, at] * dot(hidden, mine, 1, 0)

    return pl.pallas_call(
        body,
        in_specs=[pl.BlockSpec(memory_space=pltpu.SMEM)]
        + [whole() for _ in range(depth + width + 3)],
        out_specs=[whole(), whole()],
        out_shape=[like((hid, rows), jnp.float32), like((hid, part), jnp.float32)],
        compiler_params=pltpu.CompilerParams(vmem_limit_bytes=4 * MEBI),
        name="begin",
    )(rep, *grads, *hiddens, weight, slope, latent)


def backward(rep, begun, grads, rows_of, factors, weights, slopes, latents):
    gate_up, down = latents
    _, pair, hid, _ = gate_up.shape
    width = len(factors)
    depth = len(grads)
    part = grads[0].shape[1]
    block = grads[0].shape[0] // width
    flat = [*begun, *grads, *rows_of[0], *rows_of[1]]
    for triple in factors:
        flat.extend(triple)
    flat.extend([weights, *slopes, gate_up, down])

    def body(*refs):
        refs = list(refs)
        rep_ref, started_ref, dn_mine = [refs.pop(0) for _ in range(3)]
        grad_refs = [refs.pop(0) for _ in range(depth)]
        x_refs = [[refs.pop(0) for _ in range(width)] for _ in range(2)]
        triples = [[refs.pop(0) for _ in range(3)] for _ in range(width)]
        dn_weight, gu_slope, dn_slope, gu_ref, dn_ref = [refs.pop(0) for _ in range(5)]
        gu_out, dn_out, gu_new, dn_new, sems = refs
        here, there = halves(rep_ref, part)
        copies = []

        def send(source, target):
            copy = pltpu.make_async_copy(source, target, sems.at[len(copies)])
            copy.start()
            copies.append(copy)

        send(dn_mine, dn_out.at[0, :, pl.ds(here, part)])
        theirs = joined(grad_refs, block, width)
        hidden, by_gate, by_up = [
            jnp.concatenate([triple[n][...] for triple in triples], axis=1) for n in range(3)
        ]
        at = pl.ds(there, part)
        hidden_grad = started_ref[...] + dot(dn_weight[0, :, at], theirs, 1, 1)
        row_grads = jnp.concatenate(
            [(hidden_grad * factor).astype(jnp.bfloat16) for factor in (by_gate, by_up)], axis=0
        )
        for which, place in enumerate((here, there)):
            inputs = jnp.concatenate([ref[...] for ref in x_refs[which]], axis=0)
            grad = dot(row_grads, inputs, 1, 0)
            at = pl.ds(place, part)
            for i in range(pair):
                gu_new[i, which] = (
                    gu_ref[0, i, :, at] - gu_slope[0, i, :, at] * grad[i * hid : (i + 1) * hid]
                )
                send(gu_new.at[i, which], gu_out.at[0, i, :, at])
        at = pl.ds(there, part)
        dn_new[...] = dn_ref[0, :, at] - dn_slope[0, :, at] * dot(hidden, theirs, 1, 0)
        send(dn_new, dn_out.at[0, :, at])
        for copy in copies:
            copy.wait()

    return pl.pallas_call(
        body,
        in_specs=[pl.BlockSpec(memory_space=pltpu.SMEM)] + [whole() for _ in flat],
        out_specs=[pl.BlockSpec(memory_space=pl.ANY), pl.BlockSpec(memory_space=pl.ANY)],
        out_shape=[like(gate_up.shape, jnp.float32), like(down.shape, jnp.float32)],
        scratch_shapes=[
            pltpu.VMEM((pair, 2, hid, part), jnp.float32),
            pltpu.VMEM((hid, part), jnp.float32),
            pltpu.SemaphoreType.DMA((2 * pair + 2,)),
        ],
        compiler_params=pltpu.CompilerParams(vmem_limit_bytes=8 * MEBI),
        name="backward",
    )(rep, *flat)


def dense_step(tokens, teacher, expert_ids, gate_codes, gate_up_latent, down_latent):
    depth = lax.axis_size("inner")
    width = lax.axis_size("outer")
    reps = lax.axis_size("rep")
    tok_rows, part_width = tokens.shape
    rep = lax.axis_index("rep").astype(jnp.int32)[None]
    inner = lax.axis_index("inner")
    outer = lax.axis_index("outer")
    f32 = jnp.float32
    bf16 = jnp.bfloat16
    tokens, rep, inner, outer = lax.optimization_barrier((tokens, rep, inner, outer))

    def over_inner(messages, way):
        arrived = []
        for k, message in enumerate(messages):
            arrived.append(shift(message, "inner", k, way))
        return arrived

    blocks = over_inner([tokens] * depth, ahead)
    crossed = []
    for j in range(1, width):
        crossed.append(shift(tokens, "outer", j))
    gate_fan = part_width * reps
    down_fan = down_latent.shape[1] * reps
    gu_weight, blocks[0], ids, codes = per_entry(
        weight_of, [gate_up_latent], [gate_fan], bf16, carried=(tokens, expert_ids.T, gate_codes.T)
    )
    blocks[-1], gu_weight, late_down = lax.optimization_barrier(
        (blocks[-1], gu_weight, down_latent)
    )

    def code_of(column):
        expert = ahead(inner, jnp.arange(depth, dtype=jnp.int32), depth) * width + column
        chosen = ids[None] == expert[:, None, None]
        return jnp.sum(jnp.where(chosen, codes[None], 0), axis=1)

    tok_groups = [jnp.concatenate(blocks, axis=0)]
    code_groups = [code_of(outer)]
    pad_rows = -depth % 8
    rest = (depth - 1) * tok_rows
    for j in range(1, width):
        partner_codes = code_of(ahead(outer, j, width))
        pieces = jnp.concatenate([partner_codes // 256, partner_codes % 256], axis=1).astype(bf16)
        pieces = jnp.pad(pieces, ((0, pad_rows), (0, part_width - 2 * tok_rows)))
        arrived = shift(jnp.concatenate([*blocks[1:], pieces], axis=0), "outer", j)
        tok_groups.append(jnp.concatenate([crossed[j - 1], arrived[:rest]], axis=0))
        pieces = arrived[rest : rest + depth].astype(f32)
        code_groups.append(256.0 * pieces[:, :tok_rows] + pieces[:, tok_rows : 2 * tok_rows])
    gate = jnp.concatenate([c.astype(f32) for c in code_groups], axis=1) / 65536.0
    gate = upright(jnp.pad(gate, ((0, -depth % 8), (0, -gate.shape[1] % 128))))
    gate = gate[: width * tok_rows]

    (dn_weight,) = per_entry(weight_of, [late_down], [down_fan], bf16)
    their_groups, factors, keeps, arrivals = [], [], [], []
    for group in tok_groups:
        theirs = other_rep(group)
        started = project(rep, group, gu_weight)
        pre, hidden, send = forward(rep, started, theirs, gu_weight, dn_weight)
        arrivals.append(other_rep(send))
        keep, by_gate, by_up = keep_share(rep, pre, hidden, dn_weight)
        their_groups.append(theirs)
        factors.append((hidden, by_gate, by_up))
        keeps.append(keep)
    messages = list(pack(keeps, arrivals, depth))

    latents = [gate_up_latent, down_latent]
    messages[0], *latents = lax.optimization_barrier((messages[0], *latents))
    picked = over_inner(messages, back)
    slopes = per_entry(slope_of, latents, [gate_fan, down_fan], f32)
    picked[-1], *slopes = lax.optimization_barrier((picked[-1], *slopes))
    total, sent = mix(gate, picked, teacher)
    arrivals = [shift(sent, "outer", step) for step in range(1, width)]
    outgoing = upstream(gate, total, arrivals, teacher, depth)
    grads = over_inner(outgoing, ahead)
    mixed = total[:tok_rows]
    for step in range(1, width):
        source = back(0, step, width)
        mixed = mixed + arrivals[step - 1][source * tok_rows : (source + 1) * tok_rows].astype(f32)
    student_out = mixed.astype(bf16)

    their_grads = []
    for grad in grads:
        their_grads.append(other_rep(grad))
    begun = begin(rep, grads, [triple[0] for triple in factors], dn_weight, slopes[1], latents[1])
    new_gate_up, new_down = backward(
        rep,
        begun,
        their_grads,
        (tok_groups, their_groups),
        factors,
        dn_weight,
        slopes,
        latents,
    )
    return (student_out, new_gate_up, new_down)


def routed_step(tokens, teacher, expert_ids, gate_codes, gate_up_latent, down_latent):
    experts = lax.axis_size("inner") * lax.axis_size("outer")
    reps = lax.axis_size("rep")
    tok_rows, top_count = expert_ids.shape
    part_width = tokens.shape[1]
    capacity = min(tok_rows, 2 * tok_rows * top_count // experts)
    flat_ids = expert_ids.reshape(-1)
    one_hot = (flat_ids[:, None] == jnp.arange(experts, dtype=jnp.int32)[None, :]).astype(jnp.int32)
    before = jnp.cumsum(one_hot, axis=0) - one_hot
    route_slot = jnp.sum(before * one_hot, axis=1)
    target = flat_ids * capacity + route_slot
    payload = jnp.repeat(tokens, top_count, axis=0)
    outbox = jnp.zeros((experts * capacity, part_width), jnp.bfloat16).at[target].set(payload)
    received = exchange(outbox)
    expert_rows = lax.all_gather(received, "rep", axis=1, tiled=True)
    gu_weight, gu_slope = soften(gate_up_latent[0], part_width * reps)
    dn_weight, dn_slope = soften(down_latent[0], down_latent.shape[1] * reps)
    projected = lax.dot_general(
        gu_weight, expert_rows, (((2,), (1,)), ((), ())), preferred_element_type=jnp.float32
    )
    pre_gate = projected[0]
    pre_up = projected[1]
    sigmoid_gate = jax.nn.sigmoid(pre_gate)
    activated = pre_gate * sigmoid_gate
    hidden = (activated * pre_up).astype(jnp.bfloat16)
    partial_out = lax.dot_general(
        hidden, dn_weight, (((0,), (0,)), ((), ())), preferred_element_type=jnp.float32
    ).astype(jnp.bfloat16)
    rep = lax.axis_index("rep")
    keep = lax.dynamic_slice_in_dim(partial_out, rep * part_width, part_width, 1)
    send = lax.dynamic_slice_in_dim(partial_out, (1 - rep) * part_width, part_width, 1)
    expert_out = (keep.astype(jnp.float32) + other_rep(send).astype(jnp.float32)).astype(
        jnp.bfloat16
    )
    returned = exchange(expert_out)
    picked = returned[target].reshape(tok_rows, top_count, part_width)
    gating = gate_codes.astype(jnp.float32) / 65536.0
    mixed = jnp.sum(gating[:, :, None] * picked.astype(jnp.float32), axis=1)
    student_out = mixed.astype(jnp.bfloat16)
    residual = mixed - teacher.astype(jnp.float32)
    pair_grad = (
        (gating[:, :, None] * residual[:, None, :]).astype(jnp.bfloat16).reshape(-1, part_width)
    )
    grad_outbox = (
        jnp.zeros((experts * capacity, part_width), jnp.bfloat16).at[target].set(pair_grad)
    )
    grad_part = exchange(grad_outbox)
    out_grad = lax.all_gather(grad_part, "rep", axis=1, tiled=True)
    down_grad = jnp.dot(hidden, out_grad, preferred_element_type=jnp.float32)
    hidden_grad = lax.dot_general(
        dn_weight, out_grad, (((1,), (1,)), ((), ())), preferred_element_type=jnp.float32
    )
    gate_grad = (
        hidden_grad * pre_up * sigmoid_gate * (1.0 + pre_gate * (1.0 - sigmoid_gate))
    ).astype(jnp.bfloat16)
    up_grad = (hidden_grad * activated).astype(jnp.bfloat16)
    weight_grads = lax.dot_general(
        jnp.stack([gate_grad, up_grad]),
        expert_rows,
        (((2,), (0,)), ((), ())),
        preferred_element_type=jnp.float32,
    )
    new_gate_up = gate_up_latent - learn_rate * (gu_slope * weight_grads)[None]
    new_down = down_latent - learn_rate * (dn_slope * down_grad)[None]
    return (student_out, new_gate_up, new_down)


def on_device(tokens, teacher, expert_ids, gate_codes, gate_up_latent, down_latent):
    experts = lax.axis_size("inner") * lax.axis_size("outer")
    step = dense_step if expert_ids.shape[1] == experts else routed_step
    return step(tokens, teacher, expert_ids, gate_codes, gate_up_latent, down_latent)


def solution(mesh):
    return jax.shard_map(
        on_device,
        mesh=mesh,
        in_specs=(
            P(("parts", "inner", "outer"), "rep"),
            P(("parts", "inner", "outer"), "rep"),
            P(("parts", "inner", "outer"), None),
            P(("parts", "inner", "outer"), None),
            P(("inner", "outer"), None, "rep", None),
            P(("inner", "outer"), "rep", None),
        ),
        out_specs=(
            P(("parts", "inner", "outer"), "rep"),
            P(("parts", "inner", "outer"), None, "rep", None),
            P(("parts", "inner", "outer"), "rep", None),
        ),
        check_vma=False,
    )
```

```python
import math

import jax
import jax.numpy as jnp
from jax import lax
from jax.experimental import pallas as pl
from jax.experimental.pallas import tpu as pltpu
from jax.sharding import PartitionSpec as P


learn_rate = 1.0


def soft_ternary(latent):
    row_scale = jnp.mean(jnp.abs(latent), axis=-1, keepdims=True) + 1e-06
    steep = latent * (4.0 / row_scale)
    return row_scale, jnp.tanh(steep - 2.0), jnp.tanh(steep + 2.0)


def weight_of(latent, fan_in):
    row_scale, lower, upper = soft_ternary(latent)
    return (row_scale * (0.5 / math.sqrt(fan_in)) * (lower + upper)).astype(jnp.bfloat16)


def slope_of(latent, fan_in):
    _, lower, upper = soft_ternary(latent)
    root = 2.0 / math.sqrt(fan_in)
    return 2.0 * root - root * (lower * lower + upper * upper)


def soften(latent, fan_in):
    return weight_of(latent, fan_in), slope_of(latent, fan_in)


def ahead(place, step, size):
    return place ^ step if size & (size - 1) == 0 else (place + step) % size


def back(place, step, size):
    return place ^ step if size & (size - 1) == 0 else (place - step) % size


def shift(x, axis, step, way=ahead):
    size = lax.axis_size(axis)
    if step == 0:
        return x
    return lax.ppermute(x, axis, [(i, way(i, step, size)) for i in range(size)])


def other_rep(x):
    return shift(x, "rep", 1)


def exchange(outbox):
    return lax.all_to_all(outbox, ("inner", "outer"), split_axis=0, concat_axis=0, tiled=True)


MEBI = 2**20


def dot(left, right, left_dim, right_dim):
    return lax.dot_general(
        left, right, (((left_dim,), (right_dim,)), ((), ())), preferred_element_type=jnp.float32
    )


def whole():
    return pl.BlockSpec(memory_space=pltpu.VMEM)


def like(shape, dtype):
    return jax.ShapeDtypeStruct(shape, dtype)


def halves(rep_ref, part_width):
    mine = pl.multiple_of(rep_ref[0] * part_width, part_width)
    theirs = pl.multiple_of((1 - rep_ref[0]) * part_width, part_width)
    return mine, theirs


def upright(gate):
    def body(flat, tall):
        tall[...] = flat[...].T

    return pl.pallas_call(
        body,
        in_specs=[whole()],
        out_specs=whole(),
        out_shape=like(gate.shape[::-1], gate.dtype),
        compiler_params=pltpu.CompilerParams(vmem_limit_bytes=2 * MEBI),
        name="upright",
    )(gate)


def fetch(arrays):
    count = len(arrays)

    def body(*refs):
        sems = refs[-1]
        copies = [
            pltpu.make_async_copy(refs[n], refs[count + n], sems.at[n]) for n in range(count)
        ]
        for copy in copies:
            copy.start()
        for copy in copies:
            copy.wait()

    return pl.pallas_call(
        body,
        in_specs=[pl.BlockSpec(memory_space=pltpu.HBM) for _ in arrays],
        out_specs=[whole() for _ in arrays],
        out_shape=[like(array.shape, array.dtype) for array in arrays],
        scratch_shapes=[pltpu.SemaphoreType.DMA((count,))],
        compiler_params=pltpu.CompilerParams(vmem_limit_bytes=2 * MEBI),
        name="fetch",
    )(*[pltpu.with_memory_space_constraint(array, pltpu.HBM) for array in arrays])


def row_pieces(latents):
    pieces = []
    for n, latent in enumerate(latents):
        cuts = 2 if latent.shape[-2] % 32 == 0 else 1
        rows = latent.shape[-2] // cuts
        lead = [()]
        for size in latent.shape[:-2]:
            lead = [(*at, i) for at in lead for i in range(size)]
        pieces.extend((n, (*at, pl.ds(c * rows, rows))) for at in lead for c in range(cuts))
    return pieces


def weights_of(latents, fans):
    pieces = row_pieces(latents)
    count = len(latents)

    def body(*refs):
        sems = refs[-1]
        copies = []
        for slot, (n, at) in enumerate(pieces):
            copy = pltpu.make_async_copy(refs[n].at[at], refs[count + n].at[at], sems.at[slot])
            copy.start()
            copies.append(copy)
        for copy, (n, at) in zip(copies, pieces):
            copy.wait()
            refs[2 * count + n][at] = weight_of(refs[count + n][at], fans[n])

    return pl.pallas_call(
        body,
        in_specs=[pl.BlockSpec(memory_space=pltpu.HBM) for _ in latents],
        out_specs=[whole() for _ in range(2 * count)],
        out_shape=[like(latent.shape, latent.dtype) for latent in latents]
        + [like(latent.shape, jnp.bfloat16) for latent in latents],
        scratch_shapes=[pltpu.SemaphoreType.DMA((len(pieces),))],
        compiler_params=pltpu.CompilerParams(vmem_limit_bytes=4 * MEBI),
        name="weights",
    )(*[pltpu.with_memory_space_constraint(latent, pltpu.HBM) for latent in latents])


def slopes_of(latents, fans):
    pieces = row_pieces(latents)

    def body(*refs):
        for n, at in pieces:
            refs[len(latents) + n][at] = slope_of(refs[n][at], fans[n])

    return pl.pallas_call(
        body,
        in_specs=[whole() for _ in latents],
        out_specs=[whole() for _ in latents],
        out_shape=[like(latent.shape, latent.dtype) for latent in latents],
        compiler_params=pltpu.CompilerParams(vmem_limit_bytes=4 * MEBI),
        name="slopes",
    )(*latents)


def project(rep, mine, gu_weight):
    pair, hid = gu_weight.shape[1:3]
    rows, part = mine.shape

    def body(rep_ref, mine_ref, gu_ref, out):
        here, _ = halves(rep_ref, part)
        for i in range(pair):
            out[i] = dot(gu_ref[0, i, :, pl.ds(here, part)], mine_ref[...], 1, 1)

    return pl.pallas_call(
        body,
        in_specs=[pl.BlockSpec(memory_space=pltpu.SMEM), whole(), whole()],
        out_specs=whole(),
        out_shape=like((pair, hid, rows), jnp.float32),
        compiler_params=pltpu.CompilerParams(vmem_limit_bytes=4 * MEBI),
        name="project",
    )(rep, mine, gu_weight)


def forward(rep, started, theirs, gu_weight, dn_weight):
    hid = dn_weight.shape[1]
    rows, part = theirs.shape
    pair = gu_weight.shape[1]

    def body(rep_ref, started_ref, theirs_ref, gu_ref, dn_ref, pre, hidden, send):
        _, there = halves(rep_ref, part)
        at = pl.ds(there, part)
        for i in range(pair):
            pre[i] = started_ref[i] + dot(gu_ref[0, i, :, at], theirs_ref[...], 1, 1)
        pre_gate = pre[0]
        rounded = (pre_gate * jax.nn.sigmoid(pre_gate) * pre[1]).astype(jnp.bfloat16)
        hidden[...] = rounded
        send[...] = dot(rounded, dn_ref[0, :, at], 0, 0).astype(jnp.bfloat16)

    return pl.pallas_call(
        body,
        in_specs=[pl.BlockSpec(memory_space=pltpu.SMEM)] + [whole() for _ in range(4)],
        out_specs=[whole() for _ in range(3)],
        out_shape=[
            like((pair, hid, rows), jnp.float32),
            like((hid, rows), jnp.bfloat16),
            like((rows, part), jnp.bfloat16),
        ],
        compiler_params=pltpu.CompilerParams(vmem_limit_bytes=8 * MEBI),
        name="forward",
    )(rep, started, theirs, gu_weight, dn_weight)


def keep_share(rep, pre, hidden, dn_weight):
    hid, rows = hidden.shape
    part = dn_weight.shape[2] // 2

    def body(rep_ref, pre_ref, hidden_ref, dn_ref, keep, by_gate, by_up):
        here, _ = halves(rep_ref, part)
        keep[...] = dot(hidden_ref[...], dn_ref[0, :, pl.ds(here, part)], 0, 0)
        pre_gate = pre_ref[0]
        sigmoid_gate = jax.nn.sigmoid(pre_gate)
        by_gate[...] = pre_ref[1] * sigmoid_gate * (1.0 + pre_gate * (1.0 - sigmoid_gate))
        by_up[...] = pre_gate * sigmoid_gate

    return pl.pallas_call(
        body,
        in_specs=[pl.BlockSpec(memory_space=pltpu.SMEM)] + [whole() for _ in range(3)],
        out_specs=[whole() for _ in range(3)],
        out_shape=[
            like((rows, part), jnp.float32),
            like((hid, rows), jnp.float32),
            like((hid, rows), jnp.float32),
        ],
        compiler_params=pltpu.CompilerParams(vmem_limit_bytes=8 * MEBI),
        name="keep_share",
    )(rep, pre, hidden, dn_weight)


def pack(keeps, arrivals, depth):
    width = len(keeps)
    rows, part = keeps[0].shape
    block = rows // depth

    def body(*refs):
        for j in range(width):
            total = (refs[j][...] + refs[width + j][...].astype(jnp.float32)).astype(jnp.bfloat16)
            for k in range(depth):
                refs[2 * width + k][j * block : (j + 1) * block, :] = total[
                    k * block : (k + 1) * block
                ]

    return pl.pallas_call(
        body,
        in_specs=[whole() for _ in range(2 * width)],
        out_specs=[whole() for _ in range(depth)],
        out_shape=[like((width * block, part), jnp.bfloat16) for _ in range(depth)],
        compiler_params=pltpu.CompilerParams(vmem_limit_bytes=4 * MEBI),
        name="pack",
    )(*keeps, *arrivals)


def mix(gate, picked, teacher):
    rows, part = picked[0].shape
    own = teacher.shape[0]

    def body(*refs):
        gate_ref, teacher_ref = refs[:2]
        total_ref, sent_ref = refs[-2:]
        gates = gate_ref[...]
        total = 0.0
        for k, ref in enumerate(refs[2:-2]):
            total = total + gates[:, k : k + 1] * ref[...].astype(jnp.float32)
        total_ref[...] = total
        sent_ref[:own, :] = (total[:own] - teacher_ref[...].astype(jnp.float32)).astype(
            jnp.bfloat16
        )
        sent_ref[own:, :] = total[own:].astype(jnp.bfloat16)

    return pl.pallas_call(
        body,
        in_specs=[whole() for _ in range(2 + len(picked))],
        out_specs=[whole(), whole()],
        out_shape=[like((rows, part), jnp.float32), like((rows, part), jnp.bfloat16)],
        compiler_params=pltpu.CompilerParams(vmem_limit_bytes=4 * MEBI),
        name="mix",
    )(gate, teacher, *picked)


def upstream(gate, total, arrivals, teacher, depth):
    rows, part = total.shape
    own = teacher.shape[0]
    width = rows // own

    def body(*refs):
        gate_ref, teacher_ref, total_ref = refs[:3]
        arrived = refs[3 : 3 + len(arrivals)]
        outs = refs[3 + len(arrivals) :]
        gates = gate_ref[...]
        for j in range(width):
            at = slice(j * own, (j + 1) * own)
            residual = total_ref[at, :]
            for step in range(1, width):
                source = back(j, step, width)
                residual = residual + arrived[step - 1][
                    source * own : (source + 1) * own, :
                ].astype(jnp.float32)
            if j == 0:
                residual = residual - teacher_ref[...].astype(jnp.float32)
            for k in range(depth):
                outs[k][at, :] = (gates[at, k : k + 1] * residual).astype(jnp.bfloat16)

    return pl.pallas_call(
        body,
        in_specs=[whole() for _ in range(3 + len(arrivals))],
        out_specs=[whole() for _ in range(depth)],
        out_shape=[like((rows, part), jnp.bfloat16) for _ in range(depth)],
        compiler_params=pltpu.CompilerParams(vmem_limit_bytes=4 * MEBI),
        name="upstream",
    )(gate, teacher, total, *arrivals)


def joined(refs, block, width):
    return jnp.concatenate(
        [ref[j * block : (j + 1) * block, :] for j in range(width) for ref in refs], axis=0
    )


def begin(rep, grads, hiddens, weight, slope, latent):
    hid = latent.shape[1]
    width = len(hiddens)
    depth = len(grads)
    block = grads[0].shape[0] // width
    part = grads[0].shape[1]
    rows = width * depth * block

    def body(rep_ref, *refs):
        grad_refs = refs[:depth]
        hidden_refs = refs[depth : depth + width]
        weight_ref, slope_ref, latent_ref, hidden_grad, new_down = refs[depth + width :]
        here, _ = halves(rep_ref, part)
        at = pl.ds(here, part)
        mine = joined(grad_refs, block, width)
        hidden_grad[...] = dot(weight_ref[0, :, at], mine, 1, 1)
        hidden = jnp.concatenate([ref[...] for ref in hidden_refs], axis=1)
        new_down[...] = latent_ref[0, :, at] - slope_ref[0, :, at] * dot(hidden, mine, 1, 0)

    return pl.pallas_call(
        body,
        in_specs=[pl.BlockSpec(memory_space=pltpu.SMEM)]
        + [whole() for _ in range(depth + width + 3)],
        out_specs=[whole(), whole()],
        out_shape=[like((hid, rows), jnp.float32), like((hid, part), jnp.float32)],
        compiler_params=pltpu.CompilerParams(vmem_limit_bytes=4 * MEBI),
        name="begin",
    )(rep, *grads, *hiddens, weight, slope, latent)


def backward(rep, begun, grads, rows_of, factors, weights, slopes, latents):
    gate_up, down = latents
    _, pair, hid, _ = gate_up.shape
    width = len(factors)
    depth = len(grads)
    part = grads[0].shape[1]
    block = grads[0].shape[0] // width
    flat = [*begun, *grads, *rows_of[0], *rows_of[1]]
    for triple in factors:
        flat.extend(triple)
    flat.extend([weights, *slopes, gate_up, down])

    def body(*refs):
        refs = list(refs)
        rep_ref, started_ref, dn_mine = [refs.pop(0) for _ in range(3)]
        grad_refs = [refs.pop(0) for _ in range(depth)]
        x_refs = [[refs.pop(0) for _ in range(width)] for _ in range(2)]
        triples = [[refs.pop(0) for _ in range(3)] for _ in range(width)]
        dn_weight, gu_slope, dn_slope, gu_ref, dn_ref = [refs.pop(0) for _ in range(5)]
        gu_out, dn_out, gu_new, dn_new, sems = refs
        here, there = halves(rep_ref, part)
        copies = []

        def send(source, target):
            copy = pltpu.make_async_copy(source, target, sems.at[len(copies)])
            copy.start()
            copies.append(copy)

        send(dn_mine, dn_out.at[0, :, pl.ds(here, part)])
        theirs = joined(grad_refs, block, width)
        hidden, by_gate, by_up = [
            jnp.concatenate([triple[n][...] for triple in triples], axis=1) for n in range(3)
        ]
        joined_inputs = [jnp.concatenate([ref[...] for ref in refs_of], axis=0) for refs_of in x_refs]
        at = pl.ds(there, part)
        hidden_grad = started_ref[...] + dot(dn_weight[0, :, at], theirs, 1, 1)
        dn_new[...] = dn_ref[0, :, at] - dn_slope[0, :, at] * dot(hidden, theirs, 1, 0)
        send(dn_new, dn_out.at[0, :, at])
        for i, factor in enumerate((by_gate, by_up)):
            row_grad = (hidden_grad * factor).astype(jnp.bfloat16)
            for which, place in enumerate((here, there)):
                at = pl.ds(place, part)
                grad = dot(row_grad, joined_inputs[which], 1, 0)
                gu_new[i, which] = gu_ref[0, i, :, at] - gu_slope[0, i, :, at] * grad
                send(gu_new.at[i, which], gu_out.at[0, i, :, at])
        for copy in copies:
            copy.wait()

    return pl.pallas_call(
        body,
        in_specs=[pl.BlockSpec(memory_space=pltpu.SMEM)] + [whole() for _ in flat],
        out_specs=[pl.BlockSpec(memory_space=pl.ANY), pl.BlockSpec(memory_space=pl.ANY)],
        out_shape=[like(gate_up.shape, jnp.float32), like(down.shape, jnp.float32)],
        scratch_shapes=[
            pltpu.VMEM((pair, 2, hid, part), jnp.float32),
            pltpu.VMEM((hid, part), jnp.float32),
            pltpu.SemaphoreType.DMA((2 * pair + 2,)),
        ],
        compiler_params=pltpu.CompilerParams(vmem_limit_bytes=8 * MEBI),
        name="backward",
    )(rep, *flat)


def dense_step(tokens, teacher, expert_ids, gate_codes, gate_up_latent, down_latent):
    depth = lax.axis_size("inner")
    width = lax.axis_size("outer")
    reps = lax.axis_size("rep")
    tok_rows, part_width = tokens.shape
    rep = lax.axis_index("rep").astype(jnp.int32)[None]
    inner = lax.axis_index("inner")
    outer = lax.axis_index("outer")
    f32 = jnp.float32
    bf16 = jnp.bfloat16
    tokens, rep, inner, outer = lax.optimization_barrier((tokens, rep, inner, outer))

    def over_inner(messages, way):
        arrived = []
        for k, message in enumerate(messages):
            arrived.append(shift(message, "inner", k, way))
        return arrived

    blocks = over_inner([tokens] * depth, ahead)
    crossed = []
    for j in range(1, width):
        crossed.append(shift(tokens, "outer", j))
    gate_fan = part_width * reps
    down_fan = down_latent.shape[1] * reps
    blocks[0], ids, codes = fetch([tokens, expert_ids.T, gate_codes.T])
    fans = [gate_fan, down_fan]
    late = (blocks[-1], blocks[0], gate_up_latent, down_latent)
    blocks[-1], blocks[0], *latents = lax.optimization_barrier(late)

    def code_of(column):
        expert = ahead(inner, jnp.arange(depth, dtype=jnp.int32), depth) * width + column
        chosen = ids[None] == expert[:, None, None]
        return jnp.sum(jnp.where(chosen, codes[None], 0), axis=1)

    tok_groups = [jnp.concatenate(blocks, axis=0)]
    code_groups = [code_of(outer)]
    pad_rows = -depth % 8
    rest = (depth - 1) * tok_rows
    for j in range(1, width):
        partner_codes = code_of(ahead(outer, j, width))
        pieces = jnp.concatenate([partner_codes // 256, partner_codes % 256], axis=1).astype(bf16)
        pieces = jnp.pad(pieces, ((0, pad_rows), (0, part_width - 2 * tok_rows)))
        arrived = shift(jnp.concatenate([*blocks[1:], pieces], axis=0), "outer", j)
        tok_groups.append(jnp.concatenate([crossed[j - 1], arrived[:rest]], axis=0))
        pieces = arrived[rest : rest + depth].astype(f32)
        code_groups.append(256.0 * pieces[:, :tok_rows] + pieces[:, tok_rows : 2 * tok_rows])
    gate = jnp.concatenate([c.astype(f32) for c in code_groups], axis=1) / 65536.0
    gate = upright(jnp.pad(gate, ((0, -depth % 8), (0, -gate.shape[1] % 128))))
    gate = gate[: width * tok_rows]

    *latents, gu_weight, dn_weight = weights_of(latents, fans)
    their_groups, factors, keeps, arrivals = [], [], [], []
    for group in tok_groups:
        theirs = other_rep(group)
        started = project(rep, group, gu_weight)
        pre, hidden, send = forward(rep, started, theirs, gu_weight, dn_weight)
        arrivals.append(other_rep(send))
        keep, by_gate, by_up = keep_share(rep, pre, hidden, dn_weight)
        their_groups.append(theirs)
        factors.append((hidden, by_gate, by_up))
        keeps.append(keep)
    messages = list(pack(keeps, arrivals, depth))

    messages[0], *latents = lax.optimization_barrier((messages[0], *latents))
    picked = over_inner(messages, back)
    slopes = slopes_of(latents, fans)
    picked[-1], *slopes = lax.optimization_barrier((picked[-1], *slopes))
    total, sent = mix(gate, picked, teacher)
    arrivals = [shift(sent, "outer", step) for step in range(1, width)]
    outgoing = upstream(gate, total, arrivals, teacher, depth)
    grads = over_inner(outgoing, ahead)
    mixed = total[:tok_rows]
    for step in range(1, width):
        source = back(0, step, width)
        mixed = mixed + arrivals[step - 1][source * tok_rows : (source + 1) * tok_rows].astype(f32)
    student_out = mixed.astype(bf16)

    their_grads = []
    for grad in grads:
        their_grads.append(other_rep(grad))
    begun = begin(rep, grads, [triple[0] for triple in factors], dn_weight, slopes[1], latents[1])
    new_gate_up, new_down = backward(
        rep,
        begun,
        their_grads,
        (tok_groups, their_groups),
        factors,
        dn_weight,
        slopes,
        latents,
    )
    return (student_out, new_gate_up, new_down)


def routed_step(tokens, teacher, expert_ids, gate_codes, gate_up_latent, down_latent):
    experts = lax.axis_size("inner") * lax.axis_size("outer")
    reps = lax.axis_size("rep")
    tok_rows, top_count = expert_ids.shape
    part_width = tokens.shape[1]
    capacity = min(tok_rows, 2 * tok_rows * top_count // experts)
    flat_ids = expert_ids.reshape(-1)
    one_hot = (flat_ids[:, None] == jnp.arange(experts, dtype=jnp.int32)[None, :]).astype(jnp.int32)
    before = jnp.cumsum(one_hot, axis=0) - one_hot
    route_slot = jnp.sum(before * one_hot, axis=1)
    target = flat_ids * capacity + route_slot
    payload = jnp.repeat(tokens, top_count, axis=0)
    outbox = jnp.zeros((experts * capacity, part_width), jnp.bfloat16).at[target].set(payload)
    received = exchange(outbox)
    expert_rows = lax.all_gather(received, "rep", axis=1, tiled=True)
    gu_weight, gu_slope = soften(gate_up_latent[0], part_width * reps)
    dn_weight, dn_slope = soften(down_latent[0], down_latent.shape[1] * reps)
    projected = lax.dot_general(
        gu_weight, expert_rows, (((2,), (1,)), ((), ())), preferred_element_type=jnp.float32
    )
    pre_gate = projected[0]
    pre_up = projected[1]
    sigmoid_gate = jax.nn.sigmoid(pre_gate)
    activated = pre_gate * sigmoid_gate
    hidden = (activated * pre_up).astype(jnp.bfloat16)
    partial_out = lax.dot_general(
        hidden, dn_weight, (((0,), (0,)), ((), ())), preferred_element_type=jnp.float32
    ).astype(jnp.bfloat16)
    rep = lax.axis_index("rep")
    keep = lax.dynamic_slice_in_dim(partial_out, rep * part_width, part_width, 1)
    send = lax.dynamic_slice_in_dim(partial_out, (1 - rep) * part_width, part_width, 1)
    expert_out = (keep.astype(jnp.float32) + other_rep(send).astype(jnp.float32)).astype(
        jnp.bfloat16
    )
    returned = exchange(expert_out)
    picked = returned[target].reshape(tok_rows, top_count, part_width)
    gating = gate_codes.astype(jnp.float32) / 65536.0
    mixed = jnp.sum(gating[:, :, None] * picked.astype(jnp.float32), axis=1)
    student_out = mixed.astype(jnp.bfloat16)
    residual = mixed - teacher.astype(jnp.float32)
    pair_grad = (
        (gating[:, :, None] * residual[:, None, :]).astype(jnp.bfloat16).reshape(-1, part_width)
    )
    grad_outbox = (
        jnp.zeros((experts * capacity, part_width), jnp.bfloat16).at[target].set(pair_grad)
    )
    grad_part = exchange(grad_outbox)
    out_grad = lax.all_gather(grad_part, "rep", axis=1, tiled=True)
    down_grad = jnp.dot(hidden, out_grad, preferred_element_type=jnp.float32)
    hidden_grad = lax.dot_general(
        dn_weight, out_grad, (((1,), (1,)), ((), ())), preferred_element_type=jnp.float32
    )
    gate_grad = (
        hidden_grad * pre_up * sigmoid_gate * (1.0 + pre_gate * (1.0 - sigmoid_gate))
    ).astype(jnp.bfloat16)
    up_grad = (hidden_grad * activated).astype(jnp.bfloat16)
    weight_grads = lax.dot_general(
        jnp.stack([gate_grad, up_grad]),
        expert_rows,
        (((2,), (0,)), ((), ())),
        preferred_element_type=jnp.float32,
    )
    new_gate_up = gate_up_latent - learn_rate * (gu_slope * weight_grads)[None]
    new_down = down_latent - learn_rate * (dn_slope * down_grad)[None]
    return (student_out, new_gate_up, new_down)


def on_device(tokens, teacher, expert_ids, gate_codes, gate_up_latent, down_latent):
    experts = lax.axis_size("inner") * lax.axis_size("outer")
    step = dense_step if expert_ids.shape[1] == experts else routed_step
    return step(tokens, teacher, expert_ids, gate_codes, gate_up_latent, down_latent)


def solution(mesh):
    return jax.shard_map(
        on_device,
        mesh=mesh,
        in_specs=(
            P(("parts", "inner", "outer"), "rep"),
            P(("parts", "inner", "outer"), "rep"),
            P(("parts", "inner", "outer"), None),
            P(("parts", "inner", "outer"), None),
            P(("inner", "outer"), None, "rep", None),
            P(("inner", "outer"), "rep", None),
        ),
        out_specs=(
            P(("parts", "inner", "outer"), "rep"),
            P(("parts", "inner", "outer"), None, "rep", None),
            P(("parts", "inner", "outer"), "rep", None),
        ),
        check_vma=False,
    )
```

```python
import math

import jax
import jax.numpy as jnp
from jax import lax
from jax.experimental import pallas as pl
from jax.experimental.pallas import tpu as pltpu
from jax.sharding import PartitionSpec as P


learn_rate = 1.0


def soft_ternary(latent):
    row_scale = jnp.mean(jnp.abs(latent), axis=-1, keepdims=True) + 1e-06
    steep = latent * (4.0 / row_scale)
    return row_scale, jnp.tanh(steep - 2.0), jnp.tanh(steep + 2.0)


def weight_of(latent, fan_in):
    row_scale, lower, upper = soft_ternary(latent)
    return (row_scale * (0.5 / math.sqrt(fan_in)) * (lower + upper)).astype(jnp.bfloat16)


def slope_of(latent, fan_in):
    _, lower, upper = soft_ternary(latent)
    root = 2.0 / math.sqrt(fan_in)
    return 2.0 * root - root * (lower * lower + upper * upper)


def soften(latent, fan_in):
    return weight_of(latent, fan_in), slope_of(latent, fan_in)


def ahead(place, step, size):
    return place ^ step if size & (size - 1) == 0 else (place + step) % size


def back(place, step, size):
    return place ^ step if size & (size - 1) == 0 else (place - step) % size


def shift(x, axis, step, way=ahead):
    size = lax.axis_size(axis)
    if step == 0:
        return x
    return lax.ppermute(x, axis, [(i, way(i, step, size)) for i in range(size)])


def other_rep(x):
    return shift(x, "rep", 1)


def exchange(outbox):
    return lax.all_to_all(outbox, ("inner", "outer"), split_axis=0, concat_axis=0, tiled=True)


MEBI = 2**20


def dot(left, right, left_dim, right_dim):
    return lax.dot_general(
        left, right, (((left_dim,), (right_dim,)), ((), ())), preferred_element_type=jnp.float32
    )


def whole():
    return pl.BlockSpec(memory_space=pltpu.VMEM)


def like(shape, dtype):
    return jax.ShapeDtypeStruct(shape, dtype)


def halves(rep_ref, part_width):
    mine = pl.multiple_of(rep_ref[0] * part_width, part_width)
    theirs = pl.multiple_of((1 - rep_ref[0]) * part_width, part_width)
    return mine, theirs


def upright(gate):
    def body(flat, tall):
        tall[...] = flat[...].T

    return pl.pallas_call(
        body,
        in_specs=[whole()],
        out_specs=whole(),
        out_shape=like(gate.shape[::-1], gate.dtype),
        compiler_params=pltpu.CompilerParams(vmem_limit_bytes=2 * MEBI),
        name="upright",
    )(gate)


def fetch(arrays):
    count = len(arrays)

    def body(*refs):
        sems = refs[-1]
        copies = [
            pltpu.make_async_copy(refs[n], refs[count + n], sems.at[n]) for n in range(count)
        ]
        for copy in copies:
            copy.start()
        for copy in copies:
            copy.wait()

    return pl.pallas_call(
        body,
        in_specs=[pl.BlockSpec(memory_space=pltpu.HBM) for _ in arrays],
        out_specs=[whole() for _ in arrays],
        out_shape=[like(array.shape, array.dtype) for array in arrays],
        scratch_shapes=[pltpu.SemaphoreType.DMA((count,))],
        compiler_params=pltpu.CompilerParams(vmem_limit_bytes=2 * MEBI),
        name="fetch",
    )(*[pltpu.with_memory_space_constraint(array, pltpu.HBM) for array in arrays])


def row_pieces(latents):
    pieces = []
    for n, latent in enumerate(latents):
        cuts = 2 if latent.shape[-2] % 32 == 0 else 1
        rows = latent.shape[-2] // cuts
        lead = [()]
        for size in latent.shape[:-2]:
            lead = [(*at, i) for at in lead for i in range(size)]
        pieces.extend((n, (*at, pl.ds(c * rows, rows))) for at in lead for c in range(cuts))
    return pieces


def weights_of(latents, fans):
    pieces = row_pieces(latents)
    count = len(latents)

    def body(*refs):
        sems = refs[-1]
        copies = []
        for n in range(count):
            copies.append(pltpu.make_async_copy(refs[n], refs[count + n], sems.at[n]))
            copies[n].start()
        for n in range(count):
            copies[n].wait()
            for at in [at for m, at in pieces if m == n]:
                refs[2 * count + n][at] = weight_of(refs[count + n][at], fans[n])

    return pl.pallas_call(
        body,
        in_specs=[pl.BlockSpec(memory_space=pltpu.HBM) for _ in latents],
        out_specs=[whole() for _ in range(2 * count)],
        out_shape=[like(latent.shape, latent.dtype) for latent in latents]
        + [like(latent.shape, jnp.bfloat16) for latent in latents],
        scratch_shapes=[pltpu.SemaphoreType.DMA((count,))],
        compiler_params=pltpu.CompilerParams(vmem_limit_bytes=4 * MEBI),
        name="weights",
    )(*[pltpu.with_memory_space_constraint(latent, pltpu.HBM) for latent in latents])


def slopes_of(latents, fans):
    pieces = row_pieces(latents)

    def body(*refs):
        for n, at in pieces:
            refs[len(latents) + n][at] = slope_of(refs[n][at], fans[n])

    return pl.pallas_call(
        body,
        in_specs=[whole() for _ in latents],
        out_specs=[whole() for _ in latents],
        out_shape=[like(latent.shape, latent.dtype) for latent in latents],
        compiler_params=pltpu.CompilerParams(vmem_limit_bytes=4 * MEBI),
        name="slopes",
    )(*latents)


def project(rep, mine, gu_weight):
    pair, hid = gu_weight.shape[1:3]
    rows, part = mine.shape

    def body(rep_ref, mine_ref, gu_ref, out):
        here, _ = halves(rep_ref, part)
        for i in range(pair):
            out[i] = dot(gu_ref[0, i, :, pl.ds(here, part)], mine_ref[...], 1, 1)

    return pl.pallas_call(
        body,
        in_specs=[pl.BlockSpec(memory_space=pltpu.SMEM), whole(), whole()],
        out_specs=whole(),
        out_shape=like((pair, hid, rows), jnp.float32),
        compiler_params=pltpu.CompilerParams(vmem_limit_bytes=4 * MEBI),
        name="project",
    )(rep, mine, gu_weight)


def forward(rep, started, theirs, gu_weight, dn_weight):
    hid = dn_weight.shape[1]
    rows, part = theirs.shape
    pair = gu_weight.shape[1]

    def body(rep_ref, started_ref, theirs_ref, gu_ref, dn_ref, pre, hidden, send):
        _, there = halves(rep_ref, part)
        at = pl.ds(there, part)
        for i in range(pair):
            pre[i] = started_ref[i] + dot(gu_ref[0, i, :, at], theirs_ref[...], 1, 1)
        pre_gate = pre[0]
        rounded = (pre_gate * jax.nn.sigmoid(pre_gate) * pre[1]).astype(jnp.bfloat16)
        hidden[...] = rounded
        send[...] = dot(rounded, dn_ref[0, :, at], 0, 0).astype(jnp.bfloat16)

    return pl.pallas_call(
        body,
        in_specs=[pl.BlockSpec(memory_space=pltpu.SMEM)] + [whole() for _ in range(4)],
        out_specs=[whole() for _ in range(3)],
        out_shape=[
            like((pair, hid, rows), jnp.float32),
            like((hid, rows), jnp.bfloat16),
            like((rows, part), jnp.bfloat16),
        ],
        compiler_params=pltpu.CompilerParams(vmem_limit_bytes=8 * MEBI),
        name="forward",
    )(rep, started, theirs, gu_weight, dn_weight)


def keep_share(rep, pre, hidden, dn_weight):
    hid, rows = hidden.shape
    part = dn_weight.shape[2] // 2

    def body(rep_ref, pre_ref, hidden_ref, dn_ref, keep, by_gate, by_up):
        here, _ = halves(rep_ref, part)
        keep[...] = dot(hidden_ref[...], dn_ref[0, :, pl.ds(here, part)], 0, 0)
        pre_gate = pre_ref[0]
        sigmoid_gate = jax.nn.sigmoid(pre_gate)
        by_gate[...] = pre_ref[1] * sigmoid_gate * (1.0 + pre_gate * (1.0 - sigmoid_gate))
        by_up[...] = pre_gate * sigmoid_gate

    return pl.pallas_call(
        body,
        in_specs=[pl.BlockSpec(memory_space=pltpu.SMEM)] + [whole() for _ in range(3)],
        out_specs=[whole() for _ in range(3)],
        out_shape=[
            like((rows, part), jnp.float32),
            like((hid, rows), jnp.float32),
            like((hid, rows), jnp.float32),
        ],
        compiler_params=pltpu.CompilerParams(vmem_limit_bytes=8 * MEBI),
        name="keep_share",
    )(rep, pre, hidden, dn_weight)


def pack(keeps, arrivals, depth):
    width = len(keeps)
    rows, part = keeps[0].shape
    block = rows // depth

    def body(*refs):
        for j in range(width):
            total = (refs[j][...] + refs[width + j][...].astype(jnp.float32)).astype(jnp.bfloat16)
            for k in range(depth):
                refs[2 * width + k][j * block : (j + 1) * block, :] = total[
                    k * block : (k + 1) * block
                ]

    return pl.pallas_call(
        body,
        in_specs=[whole() for _ in range(2 * width)],
        out_specs=[whole() for _ in range(depth)],
        out_shape=[like((width * block, part), jnp.bfloat16) for _ in range(depth)],
        compiler_params=pltpu.CompilerParams(vmem_limit_bytes=4 * MEBI),
        name="pack",
    )(*keeps, *arrivals)


def mix(gate, picked, teacher):
    rows, part = picked[0].shape
    own = teacher.shape[0]

    def body(*refs):
        gate_ref, teacher_ref = refs[:2]
        total_ref, sent_ref = refs[-2:]
        gates = gate_ref[...]
        total = 0.0
        for k, ref in enumerate(refs[2:-2]):
            total = total + gates[:, k : k + 1] * ref[...].astype(jnp.float32)
        total_ref[...] = total
        sent_ref[:own, :] = (total[:own] - teacher_ref[...].astype(jnp.float32)).astype(
            jnp.bfloat16
        )
        sent_ref[own:, :] = total[own:].astype(jnp.bfloat16)

    return pl.pallas_call(
        body,
        in_specs=[whole() for _ in range(2 + len(picked))],
        out_specs=[whole(), whole()],
        out_shape=[like((rows, part), jnp.float32), like((rows, part), jnp.bfloat16)],
        compiler_params=pltpu.CompilerParams(vmem_limit_bytes=4 * MEBI),
        name="mix",
    )(gate, teacher, *picked)


def upstream(gate, total, arrivals, teacher, depth):
    rows, part = total.shape
    own = teacher.shape[0]
    width = rows // own

    def body(*refs):
        gate_ref, teacher_ref, total_ref = refs[:3]
        arrived = refs[3 : 3 + len(arrivals)]
        outs = refs[3 + len(arrivals) :]
        gates = gate_ref[...]
        for j in range(width):
            at = slice(j * own, (j + 1) * own)
            residual = total_ref[at, :]
            for step in range(1, width):
                source = back(j, step, width)
                residual = residual + arrived[step - 1][
                    source * own : (source + 1) * own, :
                ].astype(jnp.float32)
            if j == 0:
                residual = residual - teacher_ref[...].astype(jnp.float32)
            for k in range(depth):
                outs[k][at, :] = (gates[at, k : k + 1] * residual).astype(jnp.bfloat16)

    return pl.pallas_call(
        body,
        in_specs=[whole() for _ in range(3 + len(arrivals))],
        out_specs=[whole() for _ in range(depth)],
        out_shape=[like((rows, part), jnp.bfloat16) for _ in range(depth)],
        compiler_params=pltpu.CompilerParams(vmem_limit_bytes=4 * MEBI),
        name="upstream",
    )(gate, teacher, total, *arrivals)


def joined(refs, block, width):
    return jnp.concatenate(
        [ref[j * block : (j + 1) * block, :] for j in range(width) for ref in refs], axis=0
    )


def begin(rep, grads, hiddens, weight, slope, latent):
    hid = latent.shape[1]
    width = len(hiddens)
    depth = len(grads)
    block = grads[0].shape[0] // width
    part = grads[0].shape[1]
    rows = width * depth * block

    def body(rep_ref, *refs):
        grad_refs = refs[:depth]
        hidden_refs = refs[depth : depth + width]
        weight_ref, slope_ref, latent_ref, hidden_grad, new_down = refs[depth + width :]
        here, _ = halves(rep_ref, part)
        at = pl.ds(here, part)
        mine = joined(grad_refs, block, width)
        hidden_grad[...] = dot(weight_ref[0, :, at], mine, 1, 1)
        hidden = jnp.concatenate([ref[...] for ref in hidden_refs], axis=1)
        new_down[...] = latent_ref[0, :, at] - slope_ref[0, :, at] * dot(hidden, mine, 1, 0)

    return pl.pallas_call(
        body,
        in_specs=[pl.BlockSpec(memory_space=pltpu.SMEM)]
        + [whole() for _ in range(depth + width + 3)],
        out_specs=[whole(), whole()],
        out_shape=[like((hid, rows), jnp.float32), like((hid, part), jnp.float32)],
        compiler_params=pltpu.CompilerParams(vmem_limit_bytes=4 * MEBI),
        name="begin",
    )(rep, *grads, *hiddens, weight, slope, latent)


def backward(rep, begun, grads, rows_of, factors, weights, slopes, latents):
    gate_up, down = latents
    _, pair, hid, wide = gate_up.shape
    width = len(factors)
    depth = len(grads)
    part = grads[0].shape[1]
    block = grads[0].shape[0] // width
    flat = [*begun, *grads, *rows_of[0], *rows_of[1]]
    for triple in factors:
        flat.extend(triple)
    flat.extend([weights, *slopes, gate_up, down])

    def body(*refs):
        refs = list(refs)
        rep_ref, started_ref, dn_mine = [refs.pop(0) for _ in range(3)]
        grad_refs = [refs.pop(0) for _ in range(depth)]
        x_refs = [[refs.pop(0) for _ in range(width)] for _ in range(2)]
        triples = [[refs.pop(0) for _ in range(3)] for _ in range(width)]
        dn_weight, gu_slope, dn_slope, gu_ref, dn_ref = [refs.pop(0) for _ in range(5)]
        gu_out, dn_out, gu_new, dn_new, sems = refs
        here, there = halves(rep_ref, part)
        copies = []

        def send(source, target):
            copy = pltpu.make_async_copy(source, target, sems.at[len(copies)])
            copy.start()
            copies.append(copy)

        send(dn_mine, dn_out.at[0, :, pl.ds(here, part)])
        theirs = joined(grad_refs, block, width)
        hidden, by_gate, by_up = [
            jnp.concatenate([triple[n][...] for triple in triples], axis=1) for n in range(3)
        ]
        joined_inputs = [jnp.concatenate([ref[...] for ref in refs_of], axis=0) for refs_of in x_refs]
        at = pl.ds(there, part)
        hidden_grad = started_ref[...] + dot(dn_weight[0, :, at], theirs, 1, 1)
        dn_new[...] = dn_ref[0, :, at] - dn_slope[0, :, at] * dot(hidden, theirs, 1, 0)
        send(dn_new, dn_out.at[0, :, at])
        for i, factor in enumerate((by_gate, by_up)):
            row_grad = (hidden_grad * factor).astype(jnp.bfloat16)
            for which, place in enumerate((here, there)):
                at = pl.ds(place, part)
                grad = dot(row_grad, joined_inputs[which], 1, 0)
                gu_new[i, :, at] = gu_ref[0, i, :, at] - gu_slope[0, i, :, at] * grad
            send(gu_new.at[i], gu_out.at[0, i])
        for copy in copies:
            copy.wait()

    return pl.pallas_call(
        body,
        in_specs=[pl.BlockSpec(memory_space=pltpu.SMEM)] + [whole() for _ in flat],
        out_specs=[pl.BlockSpec(memory_space=pl.ANY), pl.BlockSpec(memory_space=pl.ANY)],
        out_shape=[like(gate_up.shape, jnp.float32), like(down.shape, jnp.float32)],
        scratch_shapes=[
            pltpu.VMEM((pair, hid, wide), jnp.float32),
            pltpu.VMEM((hid, part), jnp.float32),
            pltpu.SemaphoreType.DMA((2 * pair + 2,)),
        ],
        compiler_params=pltpu.CompilerParams(vmem_limit_bytes=8 * MEBI),
        name="backward",
    )(rep, *flat)


def dense_step(tokens, teacher, expert_ids, gate_codes, gate_up_latent, down_latent):
    depth = lax.axis_size("inner")
    width = lax.axis_size("outer")
    reps = lax.axis_size("rep")
    tok_rows, part_width = tokens.shape
    rep = lax.axis_index("rep").astype(jnp.int32)[None]
    inner = lax.axis_index("inner")
    outer = lax.axis_index("outer")
    f32 = jnp.float32
    bf16 = jnp.bfloat16
    tokens, rep, inner, outer = lax.optimization_barrier((tokens, rep, inner, outer))

    def over_inner(messages, way):
        arrived = []
        for k, message in enumerate(messages):
            arrived.append(shift(message, "inner", k, way))
        return arrived

    blocks = over_inner([tokens] * depth, ahead)
    crossed = []
    for j in range(1, width):
        crossed.append(shift(tokens, "outer", j))
    gate_fan = part_width * reps
    down_fan = down_latent.shape[1] * reps
    blocks[0], ids, codes = fetch([tokens, expert_ids.T, gate_codes.T])
    fans = [gate_fan, down_fan]
    late = (blocks[-1], blocks[0], gate_up_latent, down_latent)
    blocks[-1], blocks[0], *latents = lax.optimization_barrier(late)

    def code_of(column):
        expert = ahead(inner, jnp.arange(depth, dtype=jnp.int32), depth) * width + column
        chosen = ids[None] == expert[:, None, None]
        return jnp.sum(jnp.where(chosen, codes[None], 0), axis=1)

    tok_groups = [jnp.concatenate(blocks, axis=0)]
    code_groups = [code_of(outer)]
    pad_rows = -depth % 8
    rest = (depth - 1) * tok_rows
    for j in range(1, width):
        partner_codes = code_of(ahead(outer, j, width))
        pieces = jnp.concatenate([partner_codes // 256, partner_codes % 256], axis=1).astype(bf16)
        pieces = jnp.pad(pieces, ((0, pad_rows), (0, part_width - 2 * tok_rows)))
        arrived = shift(jnp.concatenate([*blocks[1:], pieces], axis=0), "outer", j)
        tok_groups.append(jnp.concatenate([crossed[j - 1], arrived[:rest]], axis=0))
        pieces = arrived[rest : rest + depth].astype(f32)
        code_groups.append(256.0 * pieces[:, :tok_rows] + pieces[:, tok_rows : 2 * tok_rows])
    gate = jnp.concatenate([c.astype(f32) for c in code_groups], axis=1) / 65536.0
    gate = upright(jnp.pad(gate, ((0, -depth % 8), (0, -gate.shape[1] % 128))))
    gate = gate[: width * tok_rows]

    *latents, gu_weight, dn_weight = weights_of(latents, fans)
    their_groups, factors, keeps, arrivals = [], [], [], []
    for group in tok_groups:
        theirs = other_rep(group)
        started = project(rep, group, gu_weight)
        pre, hidden, send = forward(rep, started, theirs, gu_weight, dn_weight)
        arrivals.append(other_rep(send))
        keep, by_gate, by_up = keep_share(rep, pre, hidden, dn_weight)
        their_groups.append(theirs)
        factors.append((hidden, by_gate, by_up))
        keeps.append(keep)
    messages = list(pack(keeps, arrivals, depth))

    messages[0], *latents = lax.optimization_barrier((messages[0], *latents))
    picked = over_inner(messages, back)
    slopes = slopes_of(latents, fans)
    picked[-1], *slopes = lax.optimization_barrier((picked[-1], *slopes))
    total, sent = mix(gate, picked, teacher)
    arrivals = [shift(sent, "outer", step) for step in range(1, width)]
    outgoing = upstream(gate, total, arrivals, teacher, depth)
    grads = over_inner(outgoing, ahead)
    mixed = total[:tok_rows]
    for step in range(1, width):
        source = back(0, step, width)
        mixed = mixed + arrivals[step - 1][source * tok_rows : (source + 1) * tok_rows].astype(f32)
    student_out = mixed.astype(bf16)

    their_grads = []
    for grad in grads:
        their_grads.append(other_rep(grad))
    begun = begin(rep, grads, [triple[0] for triple in factors], dn_weight, slopes[1], latents[1])
    new_gate_up, new_down = backward(
        rep,
        begun,
        their_grads,
        (tok_groups, their_groups),
        factors,
        dn_weight,
        slopes,
        latents,
    )
    return (student_out, new_gate_up, new_down)


def routed_step(tokens, teacher, expert_ids, gate_codes, gate_up_latent, down_latent):
    experts = lax.axis_size("inner") * lax.axis_size("outer")
    reps = lax.axis_size("rep")
    tok_rows, top_count = expert_ids.shape
    part_width = tokens.shape[1]
    capacity = min(tok_rows, 2 * tok_rows * top_count // experts)
    flat_ids = expert_ids.reshape(-1)
    one_hot = (flat_ids[:, None] == jnp.arange(experts, dtype=jnp.int32)[None, :]).astype(jnp.int32)
    before = jnp.cumsum(one_hot, axis=0) - one_hot
    route_slot = jnp.sum(before * one_hot, axis=1)
    target = flat_ids * capacity + route_slot
    payload = jnp.repeat(tokens, top_count, axis=0)
    outbox = jnp.zeros((experts * capacity, part_width), jnp.bfloat16).at[target].set(payload)
    received = exchange(outbox)
    expert_rows = lax.all_gather(received, "rep", axis=1, tiled=True)
    gu_weight, gu_slope = soften(gate_up_latent[0], part_width * reps)
    dn_weight, dn_slope = soften(down_latent[0], down_latent.shape[1] * reps)
    projected = lax.dot_general(
        gu_weight, expert_rows, (((2,), (1,)), ((), ())), preferred_element_type=jnp.float32
    )
    pre_gate = projected[0]
    pre_up = projected[1]
    sigmoid_gate = jax.nn.sigmoid(pre_gate)
    activated = pre_gate * sigmoid_gate
    hidden = (activated * pre_up).astype(jnp.bfloat16)
    partial_out = lax.dot_general(
        hidden, dn_weight, (((0,), (0,)), ((), ())), preferred_element_type=jnp.float32
    ).astype(jnp.bfloat16)
    rep = lax.axis_index("rep")
    keep = lax.dynamic_slice_in_dim(partial_out, rep * part_width, part_width, 1)
    send = lax.dynamic_slice_in_dim(partial_out, (1 - rep) * part_width, part_width, 1)
    expert_out = (keep.astype(jnp.float32) + other_rep(send).astype(jnp.float32)).astype(
        jnp.bfloat16
    )
    returned = exchange(expert_out)
    picked = returned[target].reshape(tok_rows, top_count, part_width)
    gating = gate_codes.astype(jnp.float32) / 65536.0
    mixed = jnp.sum(gating[:, :, None] * picked.astype(jnp.float32), axis=1)
    student_out = mixed.astype(jnp.bfloat16)
    residual = mixed - teacher.astype(jnp.float32)
    pair_grad = (
        (gating[:, :, None] * residual[:, None, :]).astype(jnp.bfloat16).reshape(-1, part_width)
    )
    grad_outbox = (
        jnp.zeros((experts * capacity, part_width), jnp.bfloat16).at[target].set(pair_grad)
    )
    grad_part = exchange(grad_outbox)
    out_grad = lax.all_gather(grad_part, "rep", axis=1, tiled=True)
    down_grad = jnp.dot(hidden, out_grad, preferred_element_type=jnp.float32)
    hidden_grad = lax.dot_general(
        dn_weight, out_grad, (((1,), (1,)), ((), ())), preferred_element_type=jnp.float32
    )
    gate_grad = (
        hidden_grad * pre_up * sigmoid_gate * (1.0 + pre_gate * (1.0 - sigmoid_gate))
    ).astype(jnp.bfloat16)
    up_grad = (hidden_grad * activated).astype(jnp.bfloat16)
    weight_grads = lax.dot_general(
        jnp.stack([gate_grad, up_grad]),
        expert_rows,
        (((2,), (0,)), ((), ())),
        preferred_element_type=jnp.float32,
    )
    new_gate_up = gate_up_latent - learn_rate * (gu_slope * weight_grads)[None]
    new_down = down_latent - learn_rate * (dn_slope * down_grad)[None]
    return (student_out, new_gate_up, new_down)


def on_device(tokens, teacher, expert_ids, gate_codes, gate_up_latent, down_latent):
    experts = lax.axis_size("inner") * lax.axis_size("outer")
    step = dense_step if expert_ids.shape[1] == experts else routed_step
    return step(tokens, teacher, expert_ids, gate_codes, gate_up_latent, down_latent)


def solution(mesh):
    return jax.shard_map(
        on_device,
        mesh=mesh,
        in_specs=(
            P(("parts", "inner", "outer"), "rep"),
            P(("parts", "inner", "outer"), "rep"),
            P(("parts", "inner", "outer"), None),
            P(("parts", "inner", "outer"), None),
            P(("inner", "outer"), None, "rep", None),
            P(("inner", "outer"), "rep", None),
        ),
        out_specs=(
            P(("parts", "inner", "outer"), "rep"),
            P(("parts", "inner", "outer"), None, "rep", None),
            P(("parts", "inner", "outer"), "rep", None),
        ),
        check_vma=False,
    )
```

```python
import math

import jax
import jax.numpy as jnp
from jax import lax
from jax.experimental import pallas as pl
from jax.experimental.pallas import tpu as pltpu
from jax.sharding import PartitionSpec as P


learn_rate = 1.0


def soft_ternary(latent):
    row_scale = jnp.mean(jnp.abs(latent), axis=-1, keepdims=True) + 1e-06
    steep = latent * (4.0 / row_scale)
    return row_scale, jnp.tanh(steep - 2.0), jnp.tanh(steep + 2.0)


def weight_of(latent, fan_in):
    row_scale, lower, upper = soft_ternary(latent)
    return (row_scale * (0.5 / math.sqrt(fan_in)) * (lower + upper)).astype(jnp.bfloat16)


def slope_of(latent, fan_in):
    _, lower, upper = soft_ternary(latent)
    root = 2.0 / math.sqrt(fan_in)
    return 2.0 * root - root * (lower * lower + upper * upper)


def soften(latent, fan_in):
    return weight_of(latent, fan_in), slope_of(latent, fan_in)


def ahead(place, step, size):
    return place ^ step if size & (size - 1) == 0 else (place + step) % size


def back(place, step, size):
    return place ^ step if size & (size - 1) == 0 else (place - step) % size


def shift(x, axis, step, way=ahead):
    size = lax.axis_size(axis)
    if step == 0:
        return x
    return lax.ppermute(x, axis, [(i, way(i, step, size)) for i in range(size)])


def other_rep(x):
    return shift(x, "rep", 1)


def exchange(outbox):
    return lax.all_to_all(outbox, ("inner", "outer"), split_axis=0, concat_axis=0, tiled=True)


MEBI = 2**20


def dot(left, right, left_dim, right_dim):
    return lax.dot_general(
        left, right, (((left_dim,), (right_dim,)), ((), ())), preferred_element_type=jnp.float32
    )


def whole():
    return pl.BlockSpec(memory_space=pltpu.VMEM)


def like(shape, dtype):
    return jax.ShapeDtypeStruct(shape, dtype)


def halves(rep_ref, part_width):
    mine = pl.multiple_of(rep_ref[0] * part_width, part_width)
    theirs = pl.multiple_of((1 - rep_ref[0]) * part_width, part_width)
    return mine, theirs


def upright(gate):
    def body(flat, tall):
        tall[...] = flat[...].T

    return pl.pallas_call(
        body,
        in_specs=[whole()],
        out_specs=whole(),
        out_shape=like(gate.shape[::-1], gate.dtype),
        compiler_params=pltpu.CompilerParams(vmem_limit_bytes=2 * MEBI),
        name="upright",
    )(gate)


def fetch(arrays):
    count = len(arrays)

    def body(*refs):
        sems = refs[-1]
        copies = [
            pltpu.make_async_copy(refs[n], refs[count + n], sems.at[n]) for n in range(count)
        ]
        for copy in copies:
            copy.start()
        for copy in copies:
            copy.wait()

    return pl.pallas_call(
        body,
        in_specs=[pl.BlockSpec(memory_space=pltpu.HBM) for _ in arrays],
        out_specs=[whole() for _ in arrays],
        out_shape=[like(array.shape, array.dtype) for array in arrays],
        scratch_shapes=[pltpu.SemaphoreType.DMA((count,))],
        compiler_params=pltpu.CompilerParams(vmem_limit_bytes=2 * MEBI),
        name="fetch",
    )(*[pltpu.with_memory_space_constraint(array, pltpu.HBM) for array in arrays])


def row_pieces(latents):
    pieces = []
    for n, latent in enumerate(latents):
        cuts = 1
        rows = latent.shape[-2] // cuts
        lead = [()]
        for size in latent.shape[:-2]:
            lead = [(*at, i) for at in lead for i in range(size)]
        pieces.extend((n, (*at, pl.ds(c * rows, rows))) for at in lead for c in range(cuts))
    return pieces


def weights_of(latents, fans):
    pieces = row_pieces(latents)
    count = len(latents)

    def body(*refs):
        sems = refs[-1]
        copies = []
        for slot, (n, at) in enumerate(pieces):
            copy = pltpu.make_async_copy(refs[n].at[at], refs[count + n].at[at], sems.at[slot])
            copy.start()
            copies.append(copy)
        for copy, (n, at) in zip(copies, pieces):
            copy.wait()
            refs[2 * count + n][at] = weight_of(refs[count + n][at], fans[n])

    return pl.pallas_call(
        body,
        in_specs=[pl.BlockSpec(memory_space=pltpu.HBM) for _ in latents],
        out_specs=[whole() for _ in range(2 * count)],
        out_shape=[like(latent.shape, latent.dtype) for latent in latents]
        + [like(latent.shape, jnp.bfloat16) for latent in latents],
        scratch_shapes=[pltpu.SemaphoreType.DMA((len(pieces),))],
        compiler_params=pltpu.CompilerParams(vmem_limit_bytes=4 * MEBI),
        name="weights",
    )(*[pltpu.with_memory_space_constraint(latent, pltpu.HBM) for latent in latents])


def slopes_of(latents, fans):
    pieces = row_pieces(latents)

    def body(*refs):
        for n, at in pieces:
            refs[len(latents) + n][at] = slope_of(refs[n][at], fans[n])

    return pl.pallas_call(
        body,
        in_specs=[whole() for _ in latents],
        out_specs=[whole() for _ in latents],
        out_shape=[like(latent.shape, latent.dtype) for latent in latents],
        compiler_params=pltpu.CompilerParams(vmem_limit_bytes=4 * MEBI),
        name="slopes",
    )(*latents)


def project(rep, mine, gu_weight):
    pair, hid = gu_weight.shape[1:3]
    rows, part = mine.shape

    def body(rep_ref, mine_ref, gu_ref, out):
        here, _ = halves(rep_ref, part)
        for i in range(pair):
            out[i] = dot(gu_ref[0, i, :, pl.ds(here, part)], mine_ref[...], 1, 1)

    return pl.pallas_call(
        body,
        in_specs=[pl.BlockSpec(memory_space=pltpu.SMEM), whole(), whole()],
        out_specs=whole(),
        out_shape=like((pair, hid, rows), jnp.float32),
        compiler_params=pltpu.CompilerParams(vmem_limit_bytes=4 * MEBI),
        name="project",
    )(rep, mine, gu_weight)


def forward(rep, started, theirs, gu_weight, dn_weight):
    hid = dn_weight.shape[1]
    rows, part = theirs.shape
    pair = gu_weight.shape[1]

    def body(rep_ref, started_ref, theirs_ref, gu_ref, dn_ref, pre, hidden, send):
        _, there = halves(rep_ref, part)
        at = pl.ds(there, part)
        for i in range(pair):
            pre[i] = started_ref[i] + dot(gu_ref[0, i, :, at], theirs_ref[...], 1, 1)
        pre_gate = pre[0]
        rounded = (pre_gate * jax.nn.sigmoid(pre_gate) * pre[1]).astype(jnp.bfloat16)
        hidden[...] = rounded
        send[...] = dot(rounded, dn_ref[0, :, at], 0, 0).astype(jnp.bfloat16)

    return pl.pallas_call(
        body,
        in_specs=[pl.BlockSpec(memory_space=pltpu.SMEM)] + [whole() for _ in range(4)],
        out_specs=[whole() for _ in range(3)],
        out_shape=[
            like((pair, hid, rows), jnp.float32),
            like((hid, rows), jnp.bfloat16),
            like((rows, part), jnp.bfloat16),
        ],
        compiler_params=pltpu.CompilerParams(vmem_limit_bytes=8 * MEBI),
        name="forward",
    )(rep, started, theirs, gu_weight, dn_weight)


def keep_share(rep, pre, hidden, dn_weight):
    hid, rows = hidden.shape
    part = dn_weight.shape[2] // 2

    def body(rep_ref, pre_ref, hidden_ref, dn_ref, keep, by_gate, by_up):
        here, _ = halves(rep_ref, part)
        keep[...] = dot(hidden_ref[...], dn_ref[0, :, pl.ds(here, part)], 0, 0)
        pre_gate = pre_ref[0]
        sigmoid_gate = jax.nn.sigmoid(pre_gate)
        by_gate[...] = pre_ref[1] * sigmoid_gate * (1.0 + pre_gate * (1.0 - sigmoid_gate))
        by_up[...] = pre_gate * sigmoid_gate

    return pl.pallas_call(
        body,
        in_specs=[pl.BlockSpec(memory_space=pltpu.SMEM)] + [whole() for _ in range(3)],
        out_specs=[whole() for _ in range(3)],
        out_shape=[
            like((rows, part), jnp.float32),
            like((hid, rows), jnp.float32),
            like((hid, rows), jnp.float32),
        ],
        compiler_params=pltpu.CompilerParams(vmem_limit_bytes=8 * MEBI),
        name="keep_share",
    )(rep, pre, hidden, dn_weight)


def pack(keeps, arrivals, depth):
    width = len(keeps)
    rows, part = keeps[0].shape
    block = rows // depth

    def body(*refs):
        for j in range(width):
            total = (refs[j][...] + refs[width + j][...].astype(jnp.float32)).astype(jnp.bfloat16)
            for k in range(depth):
                refs[2 * width + k][j * block : (j + 1) * block, :] = total[
                    k * block : (k + 1) * block
                ]

    return pl.pallas_call(
        body,
        in_specs=[whole() for _ in range(2 * width)],
        out_specs=[whole() for _ in range(depth)],
        out_shape=[like((width * block, part), jnp.bfloat16) for _ in range(depth)],
        compiler_params=pltpu.CompilerParams(vmem_limit_bytes=4 * MEBI),
        name="pack",
    )(*keeps, *arrivals)


def mix(gate, picked, teacher):
    rows, part = picked[0].shape
    own = teacher.shape[0]

    def body(*refs):
        gate_ref, teacher_ref = refs[:2]
        total_ref, sent_ref = refs[-2:]
        gates = gate_ref[...]
        total = 0.0
        for k, ref in enumerate(refs[2:-2]):
            total = total + gates[:, k : k + 1] * ref[...].astype(jnp.float32)
        total_ref[...] = total
        sent_ref[:own, :] = (total[:own] - teacher_ref[...].astype(jnp.float32)).astype(
            jnp.bfloat16
        )
        sent_ref[own:, :] = total[own:].astype(jnp.bfloat16)

    return pl.pallas_call(
        body,
        in_specs=[whole() for _ in range(2 + len(picked))],
        out_specs=[whole(), whole()],
        out_shape=[like((rows, part), jnp.float32), like((rows, part), jnp.bfloat16)],
        compiler_params=pltpu.CompilerParams(vmem_limit_bytes=4 * MEBI),
        name="mix",
    )(gate, teacher, *picked)


def upstream(gate, total, arrivals, teacher, depth):
    rows, part = total.shape
    own = teacher.shape[0]
    width = rows // own

    def body(*refs):
        gate_ref, teacher_ref, total_ref = refs[:3]
        arrived = refs[3 : 3 + len(arrivals)]
        outs = refs[3 + len(arrivals) :]
        gates = gate_ref[...]
        for j in range(width):
            at = slice(j * own, (j + 1) * own)
            residual = total_ref[at, :]
            for step in range(1, width):
                source = back(j, step, width)
                residual = residual + arrived[step - 1][
                    source * own : (source + 1) * own, :
                ].astype(jnp.float32)
            if j == 0:
                residual = residual - teacher_ref[...].astype(jnp.float32)
            for k in range(depth):
                outs[k][at, :] = (gates[at, k : k + 1] * residual).astype(jnp.bfloat16)

    return pl.pallas_call(
        body,
        in_specs=[whole() for _ in range(3 + len(arrivals))],
        out_specs=[whole() for _ in range(depth)],
        out_shape=[like((rows, part), jnp.bfloat16) for _ in range(depth)],
        compiler_params=pltpu.CompilerParams(vmem_limit_bytes=4 * MEBI),
        name="upstream",
    )(gate, teacher, total, *arrivals)


def joined(refs, block, width):
    return jnp.concatenate(
        [ref[j * block : (j + 1) * block, :] for j in range(width) for ref in refs], axis=0
    )


def begin(rep, grads, hiddens, weight, slope, latent):
    hid = latent.shape[1]
    width = len(hiddens)
    depth = len(grads)
    block = grads[0].shape[0] // width
    part = grads[0].shape[1]
    rows = width * depth * block

    def body(rep_ref, *refs):
        grad_refs = refs[:depth]
        hidden_refs = refs[depth : depth + width]
        weight_ref, slope_ref, latent_ref, hidden_grad, new_down = refs[depth + width :]
        here, _ = halves(rep_ref, part)
        at = pl.ds(here, part)
        mine = joined(grad_refs, block, width)
        hidden_grad[...] = dot(weight_ref[0, :, at], mine, 1, 1)
        hidden = jnp.concatenate([ref[...] for ref in hidden_refs], axis=1)
        new_down[...] = latent_ref[0, :, at] - slope_ref[0, :, at] * dot(hidden, mine, 1, 0)

    return pl.pallas_call(
        body,
        in_specs=[pl.BlockSpec(memory_space=pltpu.SMEM)]
        + [whole() for _ in range(depth + width + 3)],
        out_specs=[whole(), whole()],
        out_shape=[like((hid, rows), jnp.float32), like((hid, part), jnp.float32)],
        compiler_params=pltpu.CompilerParams(vmem_limit_bytes=4 * MEBI),
        name="begin",
    )(rep, *grads, *hiddens, weight, slope, latent)


def backward(rep, begun, grads, rows_of, factors, weights, slopes, latents):
    gate_up, down = latents
    _, pair, hid, wide = gate_up.shape
    width = len(factors)
    depth = len(grads)
    part = grads[0].shape[1]
    block = grads[0].shape[0] // width
    flat = [*begun, *grads, *rows_of[0], *rows_of[1]]
    for triple in factors:
        flat.extend(triple)
    flat.extend([weights, *slopes, gate_up, down])

    def body(*refs):
        refs = list(refs)
        rep_ref, started_ref, dn_mine = [refs.pop(0) for _ in range(3)]
        grad_refs = [refs.pop(0) for _ in range(depth)]
        x_refs = [[refs.pop(0) for _ in range(width)] for _ in range(2)]
        triples = [[refs.pop(0) for _ in range(3)] for _ in range(width)]
        dn_weight, gu_slope, dn_slope, gu_ref, dn_ref = [refs.pop(0) for _ in range(5)]
        gu_out, dn_out, gu_new, dn_new, sems = refs
        here, there = halves(rep_ref, part)
        copies = []

        def send(source, target):
            copy = pltpu.make_async_copy(source, target, sems.at[len(copies)])
            copy.start()
            copies.append(copy)

        send(dn_mine, dn_out.at[0, :, pl.ds(here, part)])
        theirs = joined(grad_refs, block, width)
        hidden, by_gate, by_up = [
            jnp.concatenate([triple[n][...] for triple in triples], axis=1) for n in range(3)
        ]
        joined_inputs = [jnp.concatenate([ref[...] for ref in refs_of], axis=0) for refs_of in x_refs]
        at = pl.ds(there, part)
        hidden_grad = started_ref[...] + dot(dn_weight[0, :, at], theirs, 1, 1)
        dn_new[...] = dn_ref[0, :, at] - dn_slope[0, :, at] * dot(hidden, theirs, 1, 0)
        send(dn_new, dn_out.at[0, :, at])
        for i, factor in enumerate((by_gate, by_up)):
            row_grad = (hidden_grad * factor).astype(jnp.bfloat16)
            for which, place in enumerate((here, there)):
                at = pl.ds(place, part)
                grad = dot(row_grad, joined_inputs[which], 1, 0)
                gu_new[i, :, at] = gu_ref[0, i, :, at] - gu_slope[0, i, :, at] * grad
            send(gu_new.at[i], gu_out.at[0, i])
        for copy in copies:
            copy.wait()

    return pl.pallas_call(
        body,
        in_specs=[pl.BlockSpec(memory_space=pltpu.SMEM)] + [whole() for _ in flat],
        out_specs=[pl.BlockSpec(memory_space=pl.ANY), pl.BlockSpec(memory_space=pl.ANY)],
        out_shape=[like(gate_up.shape, jnp.float32), like(down.shape, jnp.float32)],
        scratch_shapes=[
            pltpu.VMEM((pair, hid, wide), jnp.float32),
            pltpu.VMEM((hid, part), jnp.float32),
            pltpu.SemaphoreType.DMA((2 * pair + 2,)),
        ],
        compiler_params=pltpu.CompilerParams(vmem_limit_bytes=8 * MEBI),
        name="backward",
    )(rep, *flat)


def dense_step(tokens, teacher, expert_ids, gate_codes, gate_up_latent, down_latent):
    depth = lax.axis_size("inner")
    width = lax.axis_size("outer")
    reps = lax.axis_size("rep")
    tok_rows, part_width = tokens.shape
    rep = lax.axis_index("rep").astype(jnp.int32)[None]
    inner = lax.axis_index("inner")
    outer = lax.axis_index("outer")
    f32 = jnp.float32
    bf16 = jnp.bfloat16
    tokens, rep, inner, outer = lax.optimization_barrier((tokens, rep, inner, outer))

    def over_inner(messages, way):
        arrived = []
        for k, message in enumerate(messages):
            arrived.append(shift(message, "inner", k, way))
        return arrived

    blocks = over_inner([tokens] * depth, ahead)
    crossed = []
    for j in range(1, width):
        crossed.append(shift(tokens, "outer", j))
    gate_fan = part_width * reps
    down_fan = down_latent.shape[1] * reps
    blocks[0], ids, codes = fetch([tokens, expert_ids.T, gate_codes.T])
    fans = [gate_fan, down_fan]
    late = (blocks[-1], blocks[0], gate_up_latent, down_latent)
    blocks[-1], blocks[0], *latents = lax.optimization_barrier(late)

    def code_of(column):
        expert = ahead(inner, jnp.arange(depth, dtype=jnp.int32), depth) * width + column
        chosen = ids[None] == expert[:, None, None]
        return jnp.sum(jnp.where(chosen, codes[None], 0), axis=1)

    tok_groups = [jnp.concatenate(blocks, axis=0)]
    code_groups = [code_of(outer)]
    pad_rows = -depth % 8
    rest = (depth - 1) * tok_rows
    for j in range(1, width):
        partner_codes = code_of(ahead(outer, j, width))
        pieces = jnp.concatenate([partner_codes // 256, partner_codes % 256], axis=1).astype(bf16)
        pieces = jnp.pad(pieces, ((0, pad_rows), (0, part_width - 2 * tok_rows)))
        arrived = shift(jnp.concatenate([*blocks[1:], pieces], axis=0), "outer", j)
        tok_groups.append(jnp.concatenate([crossed[j - 1], arrived[:rest]], axis=0))
        pieces = arrived[rest : rest + depth].astype(f32)
        code_groups.append(256.0 * pieces[:, :tok_rows] + pieces[:, tok_rows : 2 * tok_rows])
    gate = jnp.concatenate([c.astype(f32) for c in code_groups], axis=1) / 65536.0
    gate = upright(jnp.pad(gate, ((0, -depth % 8), (0, -gate.shape[1] % 128))))
    gate = gate[: width * tok_rows]

    *latents, gu_weight, dn_weight = weights_of(latents, fans)
    their_groups, factors, keeps, arrivals = [], [], [], []
    for group in tok_groups:
        theirs = other_rep(group)
        started = project(rep, group, gu_weight)
        pre, hidden, send = forward(rep, started, theirs, gu_weight, dn_weight)
        arrivals.append(other_rep(send))
        keep, by_gate, by_up = keep_share(rep, pre, hidden, dn_weight)
        their_groups.append(theirs)
        factors.append((hidden, by_gate, by_up))
        keeps.append(keep)
    messages = list(pack(keeps, arrivals, depth))

    messages[0], *latents = lax.optimization_barrier((messages[0], *latents))
    picked = over_inner(messages, back)
    slopes = slopes_of(latents, fans)
    picked[-1], *slopes = lax.optimization_barrier((picked[-1], *slopes))
    total, sent = mix(gate, picked, teacher)
    arrivals = [shift(sent, "outer", step) for step in range(1, width)]
    outgoing = upstream(gate, total, arrivals, teacher, depth)
    grads = over_inner(outgoing, ahead)
    mixed = total[:tok_rows]
    for step in range(1, width):
        source = back(0, step, width)
        mixed = mixed + arrivals[step - 1][source * tok_rows : (source + 1) * tok_rows].astype(f32)
    student_out = mixed.astype(bf16)

    their_grads = []
    for grad in grads:
        their_grads.append(other_rep(grad))
    begun = begin(rep, grads, [triple[0] for triple in factors], dn_weight, slopes[1], latents[1])
    new_gate_up, new_down = backward(
        rep,
        begun,
        their_grads,
        (tok_groups, their_groups),
        factors,
        dn_weight,
        slopes,
        latents,
    )
    return (student_out, new_gate_up, new_down)


def routed_step(tokens, teacher, expert_ids, gate_codes, gate_up_latent, down_latent):
    experts = lax.axis_size("inner") * lax.axis_size("outer")
    reps = lax.axis_size("rep")
    tok_rows, top_count = expert_ids.shape
    part_width = tokens.shape[1]
    capacity = min(tok_rows, 2 * tok_rows * top_count // experts)
    flat_ids = expert_ids.reshape(-1)
    one_hot = (flat_ids[:, None] == jnp.arange(experts, dtype=jnp.int32)[None, :]).astype(jnp.int32)
    before = jnp.cumsum(one_hot, axis=0) - one_hot
    route_slot = jnp.sum(before * one_hot, axis=1)
    target = flat_ids * capacity + route_slot
    payload = jnp.repeat(tokens, top_count, axis=0)
    outbox = jnp.zeros((experts * capacity, part_width), jnp.bfloat16).at[target].set(payload)
    received = exchange(outbox)
    expert_rows = lax.all_gather(received, "rep", axis=1, tiled=True)
    gu_weight, gu_slope = soften(gate_up_latent[0], part_width * reps)
    dn_weight, dn_slope = soften(down_latent[0], down_latent.shape[1] * reps)
    projected = lax.dot_general(
        gu_weight, expert_rows, (((2,), (1,)), ((), ())), preferred_element_type=jnp.float32
    )
    pre_gate = projected[0]
    pre_up = projected[1]
    sigmoid_gate = jax.nn.sigmoid(pre_gate)
    activated = pre_gate * sigmoid_gate
    hidden = (activated * pre_up).astype(jnp.bfloat16)
    partial_out = lax.dot_general(
        hidden, dn_weight, (((0,), (0,)), ((), ())), preferred_element_type=jnp.float32
    ).astype(jnp.bfloat16)
    rep = lax.axis_index("rep")
    keep = lax.dynamic_slice_in_dim(partial_out, rep * part_width, part_width, 1)
    send = lax.dynamic_slice_in_dim(partial_out, (1 - rep) * part_width, part_width, 1)
    expert_out = (keep.astype(jnp.float32) + other_rep(send).astype(jnp.float32)).astype(
        jnp.bfloat16
    )
    returned = exchange(expert_out)
    picked = returned[target].reshape(tok_rows, top_count, part_width)
    gating = gate_codes.astype(jnp.float32) / 65536.0
    mixed = jnp.sum(gating[:, :, None] * picked.astype(jnp.float32), axis=1)
    student_out = mixed.astype(jnp.bfloat16)
    residual = mixed - teacher.astype(jnp.float32)
    pair_grad = (
        (gating[:, :, None] * residual[:, None, :]).astype(jnp.bfloat16).reshape(-1, part_width)
    )
    grad_outbox = (
        jnp.zeros((experts * capacity, part_width), jnp.bfloat16).at[target].set(pair_grad)
    )
    grad_part = exchange(grad_outbox)
    out_grad = lax.all_gather(grad_part, "rep", axis=1, tiled=True)
    down_grad = jnp.dot(hidden, out_grad, preferred_element_type=jnp.float32)
    hidden_grad = lax.dot_general(
        dn_weight, out_grad, (((1,), (1,)), ((), ())), preferred_element_type=jnp.float32
    )
    gate_grad = (
        hidden_grad * pre_up * sigmoid_gate * (1.0 + pre_gate * (1.0 - sigmoid_gate))
    ).astype(jnp.bfloat16)
    up_grad = (hidden_grad * activated).astype(jnp.bfloat16)
    weight_grads = lax.dot_general(
        jnp.stack([gate_grad, up_grad]),
        expert_rows,
        (((2,), (0,)), ((), ())),
        preferred_element_type=jnp.float32,
    )
    new_gate_up = gate_up_latent - learn_rate * (gu_slope * weight_grads)[None]
    new_down = down_latent - learn_rate * (dn_slope * down_grad)[None]
    return (student_out, new_gate_up, new_down)


def on_device(tokens, teacher, expert_ids, gate_codes, gate_up_latent, down_latent):
    experts = lax.axis_size("inner") * lax.axis_size("outer")
    step = dense_step if expert_ids.shape[1] == experts else routed_step
    return step(tokens, teacher, expert_ids, gate_codes, gate_up_latent, down_latent)


def solution(mesh):
    return jax.shard_map(
        on_device,
        mesh=mesh,
        in_specs=(
            P(("parts", "inner", "outer"), "rep"),
            P(("parts", "inner", "outer"), "rep"),
            P(("parts", "inner", "outer"), None),
            P(("parts", "inner", "outer"), None),
            P(("inner", "outer"), None, "rep", None),
            P(("inner", "outer"), "rep", None),
        ),
        out_specs=(
            P(("parts", "inner", "outer"), "rep"),
            P(("parts", "inner", "outer"), None, "rep", None),
            P(("parts", "inner", "outer"), "rep", None),
        ),
        check_vma=False,
    )
```
